32 devices in a mesh: groups: 2 (over y), seq: 4 (over z), chan: 2 (over x), sub: 2 (over core).
Axes of the slice: x: 2, y: 2, z: 4, core: 2. Of those that a mesh axis runs over, the one named last changes fastest.
Arguments:
- features: bfloat16 [3, 4096, 2048], P(None, ('chan', 'sub'), ('groups', 'seq')), parts along dimension 2, may hold values from -6 to 6
- dout: bfloat16 [4096, 2048], P(('chan', 'sub'), ('groups', 'seq')), parts along dimension 1, may hold values from -6 to 6
- filters: bfloat16 [4096, 1024], P(('chan', 'sub'), 'seq'), may hold values from -0.1875 to 0.1875
- taps: float32 [3, 3, 4096], P(None, None, ('chan', 'sub')), may hold values from -3.5 to 3.5
- skip: float32 [4096], P(('chan', 'sub')), may hold values from -4 to 4
- lengths: int32 [32], P('groups'), parts along dimension 0, may hold values from 1 to 256, 1024 in all
Outputs:
- out: bfloat16 [4096, 2048], P(('chan', 'sub'), ('groups', 'seq')), parts along dimension 1
- dfeatures: bfloat16 [3, 4096, 2048], P(None, ('chan', 'sub'), ('groups', 'seq')), parts along dimension 2
The draws below stay inside these ranges and needn't reach their ends.
There are 2 independent parts, one for each index of `groups`. The reference program is written for one: setup_inputs(seed, part) draws one part's arguments, and reference() takes and returns one part's arrays. A program takes and returns all parts, laid end to end along the dimension named above; an argument that names none is the same for every part. Nothing has to cross between parts.
Inputs may be any that keep to these rules, and one draw needn't show every extreme that they name: The lengths of one part sum to 1024, and the longest genome has exactly 256 positions.
All inputs are finite; a program needn't handle non-finite values.
Results may differ from the reference program's by a relative error of at most 0.01.
Values may be sent and summed in bfloat16 or wider, within the bound.
A program may use at most 64 MiB of HBM per device.

```python
import math
import jax
import jax.numpy as jnp
import numpy as np

D = 4096
TAPS = 3
GENOMES = 16
LEN = 1024
MOST = 256


def block_levels(own_key, shape, shards, low, high):
    def one(position, blocks):
        steps = jax.random.uniform(jax.random.fold_in(jax.random.fold_in(own_key, 6), position), (blocks,), jnp.float32, low / len(shards), high / len(shards))
        return jnp.repeat(jnp.exp(steps), shape[position] // blocks).reshape((-1,) + (1,) * (len(shape) - position - 1))

    loudness = one(*shards[0])
    for cut in shards[1:]:
        loudness = loudness * one(*cut)
    return loudness


def length_profile(amount, total, limit, slope):
    portions = [(1 << 20) // math.isqrt(standing ** slope) + 1 for standing in range(2, amount + 1)]
    surplus, counts = total - limit - (amount - 1), [1] * (amount - 1)
    while surplus > 0:
        free = [i for i in range(amount - 1) if counts[i] < limit]
        pool, budget = sum([portions[i] for i in free]), surplus
        for i in free:
            more = min(limit - counts[i], max(1, budget * portions[i] // pool), surplus)
            counts[i] = counts[i] + more
            surplus = surplus - more
    return np.array([limit] + counts)


def uneven(rng, amount, total, reach, skew):
    if amount == 2:
        one = jax.random.randint(rng, (), max(1, total - reach), min(reach, total - 1) + 1)
        return jnp.stack([one, total - one])
    tallies = jnp.asarray(length_profile(amount, total, reach, skew), jnp.int32)
    couples = (amount - 1) // 2
    source_of, sink = tallies[1:1 + 2 * couples:2], tallies[2:2 + 2 * couples:2]
    slack = jnp.minimum(source_of - 1, reach - sink)
    shifted = jax.random.randint(jax.random.fold_in(rng, 1), (couples,), 0, 1 << 20) % (slack + 1)
    tallies = tallies.at[1:1 + 2 * couples:2].set(source_of - shifted).at[2:2 + 2 * couples:2].set(sink + shifted)
    return tallies[jax.random.permutation(jax.random.fold_in(rng, 2), amount)]


def centred(own_key, extent, scale, reach, pieces=(), kind=jnp.bfloat16):
    array = jax.random.normal(own_key, extent, jnp.float32) * scale
    if len(pieces) > 0:
        array = block_levels(own_key, extent, pieces, -0.22, 0.18) * array
    return jnp.clip(array, min=-reach, max=reach).astype(kind)


def setup_inputs(seed: int = 0, part: int = 0) -> dict:
    key_of = jax.random.split(jax.random.key(seed), 7)
    part_keys = jax.random.split(jax.random.fold_in(key_of[6], part), 7)
    return {
        "features": centred(part_keys[0], (3, D, LEN), 1.0, 6.0, ((1, 4), (2, 4))),
        "dout": centred(part_keys[1], (D, LEN), 1.0, 6.0, ((0, 4), (1, 4))),
        "filters": centred(key_of[2], (D, LEN), LEN ** -0.5, 0.1875, ((0, 4), (1, 4))),
        "taps": centred(key_of[3], (3, TAPS, D), TAPS ** -0.5, 3.5, ((2, 4),), jnp.float32),
        "skip": centred(key_of[4], (D,), 1.0, 4.0, ((0, 4),), jnp.float32),
        "lengths": uneven(part_keys[5], GENOMES, LEN, MOST, 2).astype(jnp.int32),
    }


def genome_offsets(lengths, positions):
    ends_at = jnp.cumsum(lengths, dtype=jnp.int32)
    before = (ends_at[None, :] <= positions[:, None]).astype(jnp.int32)
    return positions - jnp.sum(before * lengths[None, :], axis=1, dtype=jnp.int32)


def short_forward(extended, taps_local, offsets):
    span_rows = offsets.shape[0]
    count = taps_local.shape[1]
    result = jnp.zeros(extended.shape[:2] + (span_rows,), jnp.float32)
    for tap_index in range(count):
        begin = count - 1 - tap_index
        window = extended[:, :, begin:begin + span_rows].astype(jnp.float32)
        keep_mask = (offsets >= tap_index).astype(jnp.float32)
        result = result + taps_local[:, tap_index, :, None] * window * keep_mask[None, None, :]
    return result


def short_backward(grads_ext, taps_local, offsets_ext):
    count = taps_local.shape[1]
    span_rows = offsets_ext.shape[0] - (count - 1)
    result = jnp.zeros(grads_ext.shape[:2] + (span_rows,), jnp.float32)
    for tap_index in range(count):
        window = grads_ext[:, :, tap_index:tap_index + span_rows]
        keep_mask = (offsets_ext[tap_index:tap_index + span_rows] >= tap_index).astype(jnp.float32)
        result = result + taps_local[:, tap_index, :, None] * window * keep_mask[None, None, :]
    return result


def reference(features, dout, filters, taps, skip, lengths):
    margin = TAPS - 1
    positions = jnp.arange(LEN, dtype=jnp.int32)
    offsets = genome_offsets(lengths, positions)
    extended = jnp.pad(features, ((0, 0), (0, 0), (margin, 0)))
    filtered = short_forward(extended, taps, offsets).astype(jnp.bfloat16)
    query_side = filtered[0].astype(jnp.float32)
    key_side = filtered[1].astype(jnp.float32)
    value_side = filtered[2].astype(jnp.float32)
    dout_f = dout.astype(jnp.float32)
    mixed = (key_side * value_side).astype(jnp.bfloat16).astype(jnp.float32)
    grad_in = (dout_f * query_side).astype(jnp.bfloat16).astype(jnp.float32)
    length_fft = 2 * LEN
    filt_spec = jnp.fft.rfft(filters.astype(jnp.float32), n=length_fft, axis=1)
    mixed_spec = jnp.fft.rfft(mixed, n=length_fft, axis=1)
    grad_spec = jnp.fft.rfft(grad_in, n=length_fft, axis=1)
    conv = jnp.fft.irfft(filt_spec * mixed_spec, n=length_fft, axis=1)[:, :LEN]
    corr = jnp.fft.irfft(jnp.conj(filt_spec) * grad_spec, n=length_fft, axis=1)[:, :LEN]
    conv = conv.astype(jnp.float32)
    corr = corr.astype(jnp.float32)
    y_out = (conv + skip[:, None] * mixed).astype(jnp.bfloat16).astype(jnp.float32)
    dmixed = (corr + skip[:, None] * grad_in).astype(jnp.bfloat16).astype(jnp.float32)
    out = (query_side * y_out).astype(jnp.bfloat16)
    grads = jnp.stack([dout_f * y_out, dmixed * value_side, dmixed * key_side])
    grads_ext = jnp.pad(grads, ((0, 0), (0, 0), (0, margin)))
    offsets_ext = genome_offsets(lengths, jnp.arange(LEN + margin, dtype=jnp.int32))
    dfeatures = short_backward(grads_ext, taps, offsets_ext).astype(jnp.bfloat16)
    return (out, dfeatures)
```

```python
import jax
import numpy as np
import jax.numpy as jnp
from jax import lax
from jax.sharding import PartitionSpec as P

HIGHEST = lax.Precision.HIGHEST
TWO_PI = 6.283185307179586


def shifted(value, axis, steps):
    count = lax.axis_size(axis)
    leading, last = (max(0, -steps), min(count, count - steps))
    return lax.ppermute(value, axis, [(source, source + steps) for source in range(leading, last)])


def genome_offsets(lengths, positions):
    ends_at = jnp.cumsum(lengths, dtype=jnp.int32)
    before = (ends_at[None, :] <= positions[:, None]).astype(jnp.int32)
    return positions - jnp.sum(before * lengths[None, :], axis=1, dtype=jnp.int32)


def short_forward(extended, taps_local, offsets):
    span_rows = offsets.shape[0]
    count = taps_local.shape[1]
    result = jnp.zeros(extended.shape[:2] + (span_rows,), jnp.float32)
    for tap_index in range(count):
        begin = count - 1 - tap_index
        window = extended[:, :, begin : begin + span_rows].astype(jnp.float32)
        keep_mask = (offsets >= tap_index).astype(jnp.float32)
        result = result + taps_local[:, tap_index, :, None] * window * keep_mask[None, None, :]
    return result


def short_backward(grads_ext, taps_local, offsets_ext):
    count = taps_local.shape[1]
    span_rows = offsets_ext.shape[0] - (count - 1)
    result = jnp.zeros(grads_ext.shape[:2] + (span_rows,), jnp.float32)
    for tap_index in range(count):
        window = grads_ext[:, :, tap_index : tap_index + span_rows]
        keep_mask = (offsets_ext[tap_index : tap_index + span_rows] >= tap_index).astype(
            jnp.float32
        )
        result = result + taps_local[:, tap_index, :, None] * window * keep_mask[None, None, :]
    return result


def dft_table(rows_n, cols_n, period):
    row_ids = jnp.arange(rows_n, dtype=jnp.int32)
    col_ids = jnp.arange(cols_n, dtype=jnp.int32)
    phase = row_ids[:, None] * col_ids[None, :] % period
    angles = phase.astype(jnp.float32) * (-TWO_PI / period)
    return (jnp.cos(angles), jnp.sin(angles))


def forward_transform(signal, tables):
    (row_re, row_im), (twid_re, twid_im), (col_re, col_im) = tables
    half_rows = signal.shape[1] // 128
    blocks_in = signal.reshape(signal.shape[0], half_rows, 128)
    part_re = jnp.einsum("kn,cnm->ckm", row_re[:, :half_rows], blocks_in, precision=HIGHEST)
    part_im = jnp.einsum("kn,cnm->ckm", row_im[:, :half_rows], blocks_in, precision=HIGHEST)
    turned_re = part_re * twid_re - part_im * twid_im
    turned_im = part_re * twid_im + part_im * twid_re
    spec_re = jnp.einsum("ckn,nm->ckm", turned_re, col_re, precision=HIGHEST) - jnp.einsum(
        "ckn,nm->ckm", turned_im, col_im, precision=HIGHEST
    )
    spec_im = jnp.einsum("ckn,nm->ckm", turned_re, col_im, precision=HIGHEST) + jnp.einsum(
        "ckn,nm->ckm", turned_im, col_re, precision=HIGHEST
    )
    return (spec_re, spec_im)


def inverse_transform(spec_re, spec_im, tables):
    (row_re, row_im), (twid_re, twid_im), (col_re, col_im) = tables
    rows_n = spec_re.shape[1]
    half_rows = rows_n // 2
    mid_re = jnp.einsum("ckn,nm->ckm", spec_re, col_re, precision=HIGHEST) + jnp.einsum(
        "ckn,nm->ckm", spec_im, col_im, precision=HIGHEST
    )
    mid_im = jnp.einsum("ckn,nm->ckm", spec_im, col_re, precision=HIGHEST) - jnp.einsum(
        "ckn,nm->ckm", spec_re, col_im, precision=HIGHEST
    )
    back_re = mid_re * twid_re + mid_im * twid_im
    back_im = mid_im * twid_re - mid_re * twid_im
    signal = jnp.einsum("nk,ckm->cnm", row_re[:half_rows], back_re, precision=HIGHEST) + jnp.einsum(
        "nk,ckm->cnm", row_im[:half_rows], back_im, precision=HIGHEST
    )
    return signal.reshape(signal.shape[0], half_rows * 128) * (1.0 / (rows_n * 128))


def long_filter(filt, mixed_in, grad_in, skip_part):
    rows_n = 2 * mixed_in.shape[1] // 128
    tables = (
        dft_table(rows_n, rows_n, rows_n),
        dft_table(rows_n, 128, rows_n * 128),
        dft_table(128, 128, 128),
    )
    mixed_f = mixed_in.astype(jnp.float32)
    grad_f = grad_in.astype(jnp.float32)
    filt_re, filt_im = forward_transform(filt.astype(jnp.float32), tables)
    mix_re, mix_im = forward_transform(mixed_f, tables)
    grad_re, grad_im = forward_transform(grad_f, tables)
    conv_out = inverse_transform(
        filt_re * mix_re - filt_im * mix_im, filt_re * mix_im + filt_im * mix_re, tables
    )
    corr_out = inverse_transform(
        filt_re * grad_re + filt_im * grad_im, filt_re * grad_im - filt_im * grad_re, tables
    )
    y_out = (conv_out + skip_part[:, None] * mixed_f).astype(jnp.bfloat16)
    dmixed = (corr_out + skip_part[:, None] * grad_f).astype(jnp.bfloat16)
    return (y_out, dmixed)


DENSE_MAX = 1024
FINE = 32


def angle_parts(length):
    base = np.arange(length, dtype=np.int64) * 4 + 1
    fine = np.arange(FINE, dtype=np.int64)[:, None] * base[None, :] % (4 * length)
    coarse = np.arange(0, length, FINE, dtype=np.int64)[:, None] * base[None, :] % (4 * length)
    scale = 2.0 * np.pi / (4 * length)
    return [
        func(part * scale).astype(np.float32)
        for part in (coarse, fine)
        for func in (np.cos, np.sin)
    ]


def dense_filter(filt, mixed_in, grad_in, skip_part):
    length = mixed_in.shape[1]
    cc, cs, fc, fs = [jnp.asarray(p)[:, None] if i < 2 else jnp.asarray(p)[None] for i, p in enumerate(angle_parts(length))]
    cos_t = (cc * fc - cs * fs).reshape(length, length)
    sin_t = (cs * fc + cc * fs).reshape(length, length)
    table = jnp.concatenate([cos_t, sin_t], axis=1).astype(jnp.bfloat16)

    def fwd(x):
        return jnp.dot(x, table, preferred_element_type=jnp.float32)

    def inv(x):
        return lax.dot_general(x.astype(jnp.bfloat16), table, (((1,), (1,)), ((), ())), preferred_element_type=jnp.float32) * (1.0 / length)

    h, m, g = fwd(filt), fwd(mixed_in), fwd(grad_in)
    hc, hs = h[:, :length], h[:, length:]
    mc, ms = m[:, :length], m[:, length:]
    gc, gs = g[:, :length], g[:, length:]
    conv_out = inv(jnp.concatenate([hc * mc - hs * ms, hc * ms + hs * mc], axis=1))
    corr_out = inv(jnp.concatenate([hc * gc + hs * gs, hc * gs - hs * gc], axis=1))
    y_out = (conv_out + skip_part[:, None] * mixed_in.astype(jnp.float32)).astype(jnp.bfloat16)
    dmixed = (corr_out + skip_part[:, None] * grad_in.astype(jnp.float32)).astype(jnp.bfloat16)
    return (y_out, dmixed)


def to_channels(stacked):
    return lax.all_to_all(stacked, "seq", split_axis=1, concat_axis=2, tiled=True)


def to_sequence(stacked):
    return lax.all_to_all(stacked, "seq", split_axis=2, concat_axis=1, tiled=True)


def local(features, dout, filters, taps, skip, lengths):
    blocks = lax.axis_size("seq")
    seq_rank = lax.axis_index("seq")
    span_rows = features.shape[2]
    channels_here = features.shape[1]
    chan_part = channels_here // blocks
    count = taps.shape[1]
    margin = count - 1
    rim = shifted(features[:, :, span_rows - margin :], "seq", 1)
    extended = jnp.concatenate([rim, features], axis=2)
    first_pos = seq_rank * span_rows
    offsets = genome_offsets(lengths, first_pos + jnp.arange(span_rows, dtype=jnp.int32))
    filtered = short_forward(extended, taps, offsets).astype(jnp.bfloat16)
    query_side = filtered[0].astype(jnp.float32)
    key_side = filtered[1].astype(jnp.float32)
    value_side = filtered[2].astype(jnp.float32)
    dout_f = dout.astype(jnp.float32)
    mixed = (key_side * value_side).astype(jnp.bfloat16)
    grad_in = (dout_f * query_side).astype(jnp.bfloat16)
    moved = to_channels(jnp.stack([mixed, grad_in, filters]))
    skip_part = lax.dynamic_slice_in_dim(skip, seq_rank * chan_part, chan_part, 0)
    run = dense_filter if moved.shape[2] <= DENSE_MAX else long_filter
    y_out, dmixed = run(moved[2], moved[0], moved[1], skip_part)
    returned = to_sequence(jnp.stack([y_out, dmixed]))
    y_here = returned[0].astype(jnp.float32)
    dmixed_here = returned[1].astype(jnp.float32)
    out = (query_side * y_here).astype(jnp.bfloat16)
    grads = jnp.stack([dout_f * y_here, dmixed_here * value_side, dmixed_here * key_side])
    ahead = shifted(grads[:, :, :margin], "seq", -1)
    grads_ext = jnp.concatenate([grads, ahead], axis=2)
    offsets_ext = genome_offsets(
        lengths, first_pos + jnp.arange(span_rows + margin, dtype=jnp.int32)
    )
    dfeatures = short_backward(grads_ext, taps, offsets_ext).astype(jnp.bfloat16)
    return (out, dfeatures)


def solution(mesh):
    in_specs = (
        P(None, ("chan", "sub"), ("groups", "seq")),
        P(("chan", "sub"), ("groups", "seq")),
        P(("chan", "sub"), "seq"),
        P(None, None, ("chan", "sub")),
        P(("chan", "sub")),
        P("groups"),
    )
    out_specs = (P(("chan", "sub"), ("groups", "seq")), P(None, ("chan", "sub"), ("groups", "seq")))
    return jax.shard_map(local, mesh=mesh, in_specs=in_specs, out_specs=out_specs, check_vma=False)
```

```python
import functools

import jax
import numpy as np
import jax.numpy as jnp
from jax import lax
from jax.experimental import pallas as pl
from jax.experimental.pallas import tpu as pltpu
from jax.sharding import PartitionSpec as P

HIGHEST = lax.Precision.HIGHEST
TWO_PI = 6.283185307179586


def shifted(value, axis, steps):
    count = lax.axis_size(axis)
    leading, last = (max(0, -steps), min(count, count - steps))
    return lax.ppermute(value, axis, [(source, source + steps) for source in range(leading, last)])


def genome_offsets(lengths, positions):
    ends_at = jnp.cumsum(lengths, dtype=jnp.int32)
    before = (ends_at[None, :] <= positions[:, None]).astype(jnp.int32)
    return positions - jnp.sum(before * lengths[None, :], axis=1, dtype=jnp.int32)


def short_forward(extended, taps_local, offsets):
    span_rows = offsets.shape[0]
    count = taps_local.shape[1]
    result = jnp.zeros(extended.shape[:2] + (span_rows,), jnp.float32)
    for tap_index in range(count):
        begin = count - 1 - tap_index
        window = extended[:, :, begin : begin + span_rows].astype(jnp.float32)
        keep_mask = (offsets >= tap_index).astype(jnp.float32)
        result = result + taps_local[:, tap_index, :, None] * window * keep_mask[None, None, :]
    return result


def short_backward(grads_ext, taps_local, offsets_ext):
    count = taps_local.shape[1]
    span_rows = offsets_ext.shape[0] - (count - 1)
    result = jnp.zeros(grads_ext.shape[:2] + (span_rows,), jnp.float32)
    for tap_index in range(count):
        window = grads_ext[:, :, tap_index : tap_index + span_rows]
        keep_mask = (offsets_ext[tap_index : tap_index + span_rows] >= tap_index).astype(
            jnp.float32
        )
        result = result + taps_local[:, tap_index, :, None] * window * keep_mask[None, None, :]
    return result


def dft_table(rows_n, cols_n, period):
    row_ids = jnp.arange(rows_n, dtype=jnp.int32)
    col_ids = jnp.arange(cols_n, dtype=jnp.int32)
    phase = row_ids[:, None] * col_ids[None, :] % period
    angles = phase.astype(jnp.float32) * (-TWO_PI / period)
    return (jnp.cos(angles), jnp.sin(angles))


def forward_transform(signal, tables):
    (row_re, row_im), (twid_re, twid_im), (col_re, col_im) = tables
    half_rows = signal.shape[1] // 128
    blocks_in = signal.reshape(signal.shape[0], half_rows, 128)
    part_re = jnp.einsum("kn,cnm->ckm", row_re[:, :half_rows], blocks_in, precision=HIGHEST)
    part_im = jnp.einsum("kn,cnm->ckm", row_im[:, :half_rows], blocks_in, precision=HIGHEST)
    turned_re = part_re * twid_re - part_im * twid_im
    turned_im = part_re * twid_im + part_im * twid_re
    spec_re = jnp.einsum("ckn,nm->ckm", turned_re, col_re, precision=HIGHEST) - jnp.einsum(
        "ckn,nm->ckm", turned_im, col_im, precision=HIGHEST
    )
    spec_im = jnp.einsum("ckn,nm->ckm", turned_re, col_im, precision=HIGHEST) + jnp.einsum(
        "ckn,nm->ckm", turned_im, col_re, precision=HIGHEST
    )
    return (spec_re, spec_im)


def inverse_transform(spec_re, spec_im, tables):
    (row_re, row_im), (twid_re, twid_im), (col_re, col_im) = tables
    rows_n = spec_re.shape[1]
    half_rows = rows_n // 2
    mid_re = jnp.einsum("ckn,nm->ckm", spec_re, col_re, precision=HIGHEST) + jnp.einsum(
        "ckn,nm->ckm", spec_im, col_im, precision=HIGHEST
    )
    mid_im = jnp.einsum("ckn,nm->ckm", spec_im, col_re, precision=HIGHEST) - jnp.einsum(
        "ckn,nm->ckm", spec_re, col_im, precision=HIGHEST
    )
    back_re = mid_re * twid_re + mid_im * twid_im
    back_im = mid_im * twid_re - mid_re * twid_im
    signal = jnp.einsum("nk,ckm->cnm", row_re[:half_rows], back_re, precision=HIGHEST) + jnp.einsum(
        "nk,ckm->cnm", row_im[:half_rows], back_im, precision=HIGHEST
    )
    return signal.reshape(signal.shape[0], half_rows * 128) * (1.0 / (rows_n * 128))


def long_filter(filt, mixed_in, grad_in, skip_part):
    rows_n = 2 * mixed_in.shape[1] // 128
    tables = (
        dft_table(rows_n, rows_n, rows_n),
        dft_table(rows_n, 128, rows_n * 128),
        dft_table(128, 128, 128),
    )
    mixed_f = mixed_in.astype(jnp.float32)
    grad_f = grad_in.astype(jnp.float32)
    filt_re, filt_im = forward_transform(filt.astype(jnp.float32), tables)
    mix_re, mix_im = forward_transform(mixed_f, tables)
    grad_re, grad_im = forward_transform(grad_f, tables)
    conv_out = inverse_transform(
        filt_re * mix_re - filt_im * mix_im, filt_re * mix_im + filt_im * mix_re, tables
    )
    corr_out = inverse_transform(
        filt_re * grad_re + filt_im * grad_im, filt_re * grad_im - filt_im * grad_re, tables
    )
    y_out = (conv_out + skip_part[:, None] * mixed_f).astype(jnp.bfloat16)
    dmixed = (corr_out + skip_part[:, None] * grad_f).astype(jnp.bfloat16)
    return (y_out, dmixed)


DENSE_MAX = 1024
FINE = 32


def angle_parts(length):
    base = np.arange(length, dtype=np.int64) * 4 + 1
    fine = np.arange(FINE, dtype=np.int64)[:, None] * base[None, :] % (4 * length)
    coarse = np.arange(0, length, FINE, dtype=np.int64)[:, None] * base[None, :] % (4 * length)
    scale = 2.0 * np.pi / (4 * length)
    return [
        func(part * scale).astype(np.float32)
        for part in (coarse, fine)
        for func in (np.cos, np.sin)
    ]


def dense_filter(filt, mixed_in, grad_in, skip_part):
    length = mixed_in.shape[1]
    cc, cs, fc, fs = [jnp.asarray(p)[:, None] if i < 2 else jnp.asarray(p)[None] for i, p in enumerate(angle_parts(length))]
    cos_t = (cc * fc - cs * fs).reshape(length, length)
    sin_t = (cs * fc + cc * fs).reshape(length, length)
    table = jnp.concatenate([cos_t, sin_t], axis=1).astype(jnp.bfloat16)

    def fwd(x):
        return jnp.dot(x, table, preferred_element_type=jnp.float32)

    def inv(x):
        return lax.dot_general(x.astype(jnp.bfloat16), table, (((1,), (1,)), ((), ())), preferred_element_type=jnp.float32) * (1.0 / length)

    h, m, g = fwd(filt), fwd(mixed_in), fwd(grad_in)
    hc, hs = h[:, :length], h[:, length:]
    mc, ms = m[:, :length], m[:, length:]
    gc, gs = g[:, :length], g[:, length:]
    conv_out = inv(jnp.concatenate([hc * mc - hs * ms, hc * ms + hs * mc], axis=1))
    corr_out = inv(jnp.concatenate([hc * gc + hs * gs, hc * gs - hs * gc], axis=1))
    y_out = (conv_out + skip_part[:, None] * mixed_in.astype(jnp.float32)).astype(jnp.bfloat16)
    dmixed = (corr_out + skip_part[:, None] * grad_in.astype(jnp.float32)).astype(jnp.bfloat16)
    return (y_out, dmixed)


def to_channels(stacked):
    return lax.all_to_all(stacked, "seq", split_axis=1, concat_axis=2, tiled=True)


def to_sequence(stacked):
    return lax.all_to_all(stacked, "seq", split_axis=2, concat_axis=1, tiled=True)


def local_general(features, dout, filters, taps, skip, lengths):
    blocks = lax.axis_size("seq")
    seq_rank = lax.axis_index("seq")
    span_rows = features.shape[2]
    channels_here = features.shape[1]
    chan_part = channels_here // blocks
    count = taps.shape[1]
    margin = count - 1
    rim = shifted(features[:, :, span_rows - margin :], "seq", 1)
    extended = jnp.concatenate([rim, features], axis=2)
    first_pos = seq_rank * span_rows
    offsets = genome_offsets(lengths, first_pos + jnp.arange(span_rows, dtype=jnp.int32))
    filtered = short_forward(extended, taps, offsets).astype(jnp.bfloat16)
    query_side = filtered[0].astype(jnp.float32)
    key_side = filtered[1].astype(jnp.float32)
    value_side = filtered[2].astype(jnp.float32)
    dout_f = dout.astype(jnp.float32)
    mixed = (key_side * value_side).astype(jnp.bfloat16)
    grad_in = (dout_f * query_side).astype(jnp.bfloat16)
    moved = to_channels(jnp.stack([mixed, grad_in, filters]))
    skip_part = lax.dynamic_slice_in_dim(skip, seq_rank * chan_part, chan_part, 0)
    run = dense_filter if moved.shape[2] <= DENSE_MAX else long_filter
    y_out, dmixed = run(moved[2], moved[0], moved[1], skip_part)
    returned = to_sequence(jnp.stack([y_out, dmixed]))
    y_here = returned[0].astype(jnp.float32)
    dmixed_here = returned[1].astype(jnp.float32)
    out = (query_side * y_here).astype(jnp.bfloat16)
    grads = jnp.stack([dout_f * y_here, dmixed_here * value_side, dmixed_here * key_side])
    ahead = shifted(grads[:, :, :margin], "seq", -1)
    grads_ext = jnp.concatenate([grads, ahead], axis=2)
    offsets_ext = genome_offsets(
        lengths, first_pos + jnp.arange(span_rows + margin, dtype=jnp.int32)
    )
    dfeatures = short_backward(grads_ext, taps, offsets_ext).astype(jnp.bfloat16)
    return (out, dfeatures)


HALF = 128
NN = (((1,), (0,)), ((), ()))
NT = (((1,), (1,)), ((), ()))
TN = (((0,), (0,)), ((), ()))


def mm(a, b, dims=NN):
    return lax.dot_general(a, b, dims, preferred_element_type=jnp.float32)


def mixer_kernel(
    n,
    lengths_ref, feat_ref, dout_ref, filt_ref, par_ref, tab_ref,
    out_ref, df_ref,
    rim_src, rim, shift_m, place, keep_s, q_s, k_s, v_s, d_s,
    fwd_send, fwd_recv, filt_recv, table, spec_h, spec, y_send, y_recv, hal_src, hal,
    rim_ss, rim_rs, filt_ss, filt_rs, fwd_ss, fwd_rs, y_ss, y_rs, hal_ss, hal_rs,
):
    rank = lax.axis_index("seq")
    span = feat_ref.shape[2]
    part = feat_ref.shape[1] // n
    subs = part // HALF
    length = span * n
    wide = span + 128
    bf = jnp.bfloat16
    f32 = jnp.float32

    def peer(step):
        return lax.rem(rank + 1 + step, n)

    barrier = pltpu.get_barrier_semaphore()
    for step in range(n - 1):
        pl.semaphore_signal(barrier, inc=1, device_id={"seq": peer(step)}, device_id_type=pl.DeviceIdType.MESH)

    def remote(src, dst, ss, rs, dest):
        return pltpu.make_async_remote_copy(
            src_ref=src, dst_ref=dst, send_sem=ss, recv_sem=rs,
            device_id={"seq": dest}, device_id_type=pl.DeviceIdType.MESH,
        )

    def rim_copy(side, dest):
        return remote(rim_src, rim.at[pl.ds(16 * side, 16)], rim_ss.at[side], rim_rs.at[side], dest)

    def filt_copy(who, dest):
        rows = pl.ds(pl.multiple_of(dest * part, HALF), part)
        cols = pl.ds(pl.multiple_of(who * span, 128), span)
        return remote(filt_ref.at[rows], filt_recv.at[:, cols], filt_ss.at[dest], filt_rs.at[who], dest)

    def fwd_copy(sub, who, dest):
        cols = pl.ds(pl.multiple_of(who * span, 128), span)
        return remote(fwd_send.at[sub, dest], fwd_recv.at[sub, :, cols], fwd_ss.at[sub, dest], fwd_rs.at[sub, who], dest)

    def y_copy(sub, who, dest):
        return remote(y_send.at[sub, dest], y_recv.at[sub, who], y_ss.at[sub, dest], y_rs.at[sub, who], dest)

    def hal_copy(sub, dest):
        return remote(hal_src.at[sub], hal.at[sub], hal_ss.at[sub], hal_rs.at[sub], dest)

    r_id = lax.broadcasted_iota(jnp.int32, (16, span), 0)
    p_id = lax.broadcasted_iota(jnp.int32, (16, span), 1)
    total = None
    for a in range(4):
        hit = (
            ((r_id == 4 * a) & (p_id == span - 2)) | ((r_id == 4 * a + 1) & (p_id == span - 1))
            | ((r_id == 4 * a + 2) & (p_id == 0)) | ((r_id == 4 * a + 3) & (p_id == 1))
        )
        pick = jnp.where(hit, 1.0, 0.0).astype(bf)
        term = mm(pick, feat_ref[a] if a < 3 else dout_ref[...], NT)
        total = term if total is None else total + term
    rim_src[...] = total.astype(bf)

    @pl.when(rank == 0)
    def _():
        rim[0:16, :] = jnp.zeros((16, rim.shape[1]), bf)

    @pl.when(rank == n - 1)
    def _():
        rim[16:32, :] = jnp.zeros((16, rim.shape[1]), bf)
        for sub in range(subs):
            hal[sub] = jnp.zeros(hal.shape[1:], bf)

    pl.semaphore_wait(barrier, n - 1)

    @pl.when(rank < n - 1)
    def _():
        rim_copy(0, rank + 1).start()

    @pl.when(rank > 0)
    def _():
        rim_copy(1, rank - 1).start()

    for step in range(n - 1):
        filt_copy(rank, peer(step)).start()
    mine = pl.ds(pl.multiple_of(rank * span, 128), span)
    filt_recv[:, mine] = filt_ref[pl.ds(pl.multiple_of(rank * part, HALF), part), :]

    def offsets_of(ahead, width):
        position = rank * span + ahead + lax.broadcasted_iota(jnp.int32, (8, width), 1)
        result = position
        end = jnp.int32(0)
        for g in range(lengths_ref.shape[0]):
            one = lengths_ref[g]
            end = end + one
            result = result - jnp.where(end <= position, one, 0)
        return result

    off_wide = offsets_of(0, wide)
    keep_s[0] = jnp.where(offsets_of(1, span) >= 1, 1.0, 0.0)
    keep_s[1] = jnp.where(offsets_of(2, span) >= 2, 1.0, 0.0)
    src_id = lax.broadcasted_iota(jnp.int32, (span, wide), 0)
    dst_id = lax.broadcasted_iota(jnp.int32, (span, wide), 1)
    row_id = lax.broadcasted_iota(jnp.int32, (32, wide), 0)
    col_id = lax.broadcasted_iota(jnp.int32, (32, wide), 1)
    for j in range(3):
        keep = jnp.where(off_wide >= j, 1.0, 0.0)[0:1, :]
        shift_m[j] = (jnp.where(dst_id - j == src_id, 1.0, 0.0) * keep).astype(bf)
        for a in range(4):
            hit = (
                ((row_id == 4 * a) & (col_id - j == -2)) | ((row_id == 4 * a + 1) & (col_id - j == -1))
                | ((row_id == 16 + 4 * a + 2) & (col_id - j == span))
                | ((row_id == 16 + 4 * a + 3) & (col_id - j == span + 1))
            )
            place[a, j] = (jnp.where(hit, 1.0, 0.0) * keep).astype(bf)

    @pl.when(rank > 0)
    def _():
        rim_copy(0, rank).wait_recv()

    @pl.when(rank < n - 1)
    def _():
        rim_copy(1, rank).wait_recv()

    def prepare(index, carry):
        sub = index // n
        dest = lax.rem(rank + 1 + lax.rem(index, n), n)
        first = pl.multiple_of(dest * part + sub * HALF, HALF)
        rows = pl.ds(first, HALF)
        rim_part = rim[:, rows]
        par = par_ref[rows, :]

        def shifted_in(a, j):
            source = feat_ref[a, rows, :] if a < 3 else dout_ref[rows, :]
            return mm(source, shift_m[j]) + mm(rim_part, place[a, j], TN)

        result = []
        for a in range(3):
            acc = par[:, 3 * a : 3 * a + 1] * shifted_in(a, 0)
            acc = acc + par[:, 3 * a + 1 : 3 * a + 2] * shifted_in(a, 1)
            acc = acc + par[:, 3 * a + 2 : 3 * a + 3] * shifted_in(a, 2)
            result.append(acc.astype(bf))
        d_wide = shifted_in(3, 0).astype(bf)
        q_s[rows, :] = result[0][:, :span]
        k_s[rows, :] = result[1]
        v_s[rows, :] = result[2]
        d_s[rows, :] = d_wide
        mixed = (result[1][:, :span].astype(f32) * result[2][:, :span].astype(f32)).astype(bf)
        grad_in = (d_wide[:, :span].astype(f32) * result[0][:, :span].astype(f32)).astype(bf)

        @pl.when(dest != rank)
        def _():
            fwd_send[sub, dest, 0:HALF, :] = mixed
            fwd_send[sub, dest, HALF:, :] = grad_in
            fwd_copy(sub, rank, dest).start()

        @pl.when(dest == rank)
        def _():
            fwd_recv[sub, 0:HALF, mine] = mixed
            fwd_recv[sub, HALF:, mine] = grad_in

        return carry

    lax.fori_loop(0, n * subs, prepare, 0)

    fine_c = tab_ref[2]
    fine_s = tab_ref[3]

    def build(a, carry):
        big_c = tab_ref[0, pl.ds(a, 1), :]
        big_s = tab_ref[1, pl.ds(a, 1), :]
        rows = pl.ds(pl.multiple_of(a * FINE, FINE), FINE)
        table[rows, 0:length] = (big_c * fine_c - big_s * fine_s).astype(bf)
        table[rows, length:] = (big_s * fine_c + big_c * fine_s).astype(bf)
        return carry

    lax.fori_loop(0, length // FINE, build, 0)

    for step in range(n - 1):
        filt_copy(peer(step), rank).wait_recv()

    tile = 256

    def filter_tile(t, carry):
        cols = pl.ds(pl.multiple_of(t * tile, tile), tile)
        spec_h[:, cols] = mm(filt_recv[...], table[:, cols])
        return carry

    lax.fori_loop(0, 2 * length // tile, filter_tile, 0)

    for sub in range(subs):
        for step in range(n - 1):
            fwd_copy(sub, peer(step), rank).wait_recv()
        h_rows = pl.ds(sub * HALF, HALF)

        def spectrum_tile(t, carry):
            cols = pl.ds(pl.multiple_of(t * tile, tile), tile)
            sins = pl.ds(pl.multiple_of(length + t * tile, tile), tile)
            signal = fwd_recv[sub]
            x_c = mm(signal, table[:, cols])
            x_s = mm(signal, table[:, sins])
            h_c = spec_h[h_rows, cols]
            h_s = spec_h[h_rows, sins]
            spec[0:HALF, cols] = (h_c * x_c[:HALF] - h_s * x_s[:HALF]).astype(bf)
            spec[0:HALF, sins] = (h_c * x_s[:HALF] + h_s * x_c[:HALF]).astype(bf)
            spec[HALF:, cols] = (h_c * x_c[HALF:] + h_s * x_s[HALF:]).astype(bf)
            spec[HALF:, sins] = (h_c * x_s[HALF:] - h_s * x_c[HALF:]).astype(bf)
            return carry

        lax.fori_loop(0, length // tile, spectrum_tile, 0)
        skip_col = par_ref[pl.ds(pl.multiple_of(rank * part + sub * HALF, HALF), HALF), 9:10]

        def give_back(step, carry):
            dest = lax.rem(rank + 1 + step, n)
            block = pl.ds(pl.multiple_of(dest * span, 128), span)
            value = mm(spec[...], table[block, :], NT) * (1.0 / length)
            signal = fwd_recv[sub, :, block].astype(f32)
            y_part = (value[:HALF] + skip_col * signal[:HALF]).astype(bf)
            d_part = (value[HALF:] + skip_col * signal[HALF:]).astype(bf)

            @pl.when(dest != rank)
            def _():
                y_send[sub, dest, 0:HALF, :] = y_part
                y_send[sub, dest, HALF:, :] = d_part
                y_copy(sub, rank, dest).start()

            @pl.when(dest == rank)
            def _():
                y_recv[sub, rank, 0:HALF, :] = y_part
                y_recv[sub, rank, HALF:, :] = d_part

            return carry

        lax.fori_loop(0, n, give_back, 0)

    r_id = lax.broadcasted_iota(jnp.int32, (16, 128), 0)
    c_id = lax.broadcasted_iota(jnp.int32, (16, 128), 1)
    eye = jnp.where((r_id == c_id) & (r_id < 2), 1.0, 0.0).astype(bf)

    def halo_send(sub):
        for step in range(n - 1):
            y_copy(sub, peer(step), rank).wait_recv()
        for s in range(n):
            hal_src[sub, :, s * 2 * HALF : (s + 1) * 2 * HALF] = mm(eye, y_recv[sub, s, :, 0:128], NT).astype(bf)

        @pl.when(rank > 0)
        def _():
            hal_copy(sub, rank - 1).start()

    def finish(sub):
        @pl.when(rank < n - 1)
        def _():
            hal_copy(sub, rank).wait_recv()

        def rows_of(s, carry):
            rows = pl.ds(pl.multiple_of(s * part + sub * HALF, HALF), HALF)
            par = par_ref[rows, :]
            y_rim = mm(hal[sub, :, pl.ds(pl.multiple_of(s * 2 * HALF, HALF), HALF)], eye, TN)
            d_rim = mm(hal[sub, :, pl.ds(pl.multiple_of(s * 2 * HALF + HALF, HALF), HALF)], eye, TN)
            y_here = y_recv[sub, s, 0:HALF, :].astype(f32)
            d_here = y_recv[sub, s, HALF:, :].astype(f32)
            out_ref[rows, :] = (q_s[rows, :].astype(f32) * y_here).astype(bf)
            y_wide = jnp.concatenate([y_here, y_rim], axis=1)
            d_wide = jnp.concatenate([d_here, d_rim], axis=1)
            for c in range(3):
                if c == 0:
                    grads = d_s[rows, :].astype(f32) * y_wide
                elif c == 1:
                    grads = d_wide * v_s[rows, :].astype(f32)
                else:
                    grads = d_wide * k_s[rows, :].astype(f32)
                acc = par[:, 3 * c : 3 * c + 1] * grads[:, :span]
                for j in (1, 2):
                    moved = pltpu.roll(grads, wide - j, 1)[:, :span]
                    acc = acc + par[:, 3 * c + j : 3 * c + j + 1] * moved * keep_s[j - 1, 0:1, :]
                df_ref[c, rows, :] = acc.astype(bf)
            return carry

        lax.fori_loop(0, n, rows_of, 0)

    for sub in range(subs):
        halo_send(sub)
        if sub > 0:
            finish(sub - 1)
    finish(subs - 1)

    @pl.when(rank < n - 1)
    def _():
        rim_copy(0, rank).wait_send()

    @pl.when(rank > 0)
    def _():
        rim_copy(1, rank).wait_send()
        for sub in range(subs):
            hal_copy(sub, rank).wait_send()

    for step in range(n - 1):
        filt_copy(rank, peer(step)).wait_send()
        for sub in range(subs):
            fwd_copy(sub, rank, peer(step)).wait_send()
            y_copy(sub, rank, peer(step)).wait_send()


def local_kernel(features, dout, filters, taps, skip, lengths):
    n = lax.axis_size("seq")
    channels, span = dout.shape
    part = channels // n
    subs = part // HALF
    length = n * span
    wide = span + 128
    bf = jnp.bfloat16
    par = jnp.concatenate([taps.reshape(9, channels), skip[None]], axis=0).T
    tab = jnp.asarray(np.stack(angle_parts(length)))
    vmem = pl.BlockSpec(memory_space=pltpu.VMEM)
    dma = pltpu.SemaphoreType.DMA
    return pl.pallas_call(
        functools.partial(mixer_kernel, n),
        out_shape=(
            jax.ShapeDtypeStruct(dout.shape, bf),
            jax.ShapeDtypeStruct(features.shape, bf),
        ),
        in_specs=[pl.BlockSpec(memory_space=pltpu.SMEM)] + [vmem] * 5,
        out_specs=(vmem, vmem),
        scratch_shapes=[
            pltpu.VMEM((16, channels), bf),
            pltpu.VMEM((32, channels), bf),
            pltpu.VMEM((3, span, wide), bf),
            pltpu.VMEM((4, 3, 32, wide), bf),
            pltpu.VMEM((2, 8, span), jnp.float32),
            pltpu.VMEM((channels, span), bf),
            pltpu.VMEM((channels, wide), bf),
            pltpu.VMEM((channels, wide), bf),
            pltpu.VMEM((channels, wide), bf),
            pltpu.VMEM((subs, n, 2 * HALF, span), bf),
            pltpu.VMEM((subs, 2 * HALF, length), bf),
            pltpu.VMEM((part, length), bf),
            pltpu.VMEM((length, 2 * length), bf),
            pltpu.VMEM((part, 2 * length), jnp.float32),
            pltpu.VMEM((2 * HALF, 2 * length), bf),
            pltpu.VMEM((subs, n, 2 * HALF, span), bf),
            pltpu.VMEM((subs, n, 2 * HALF, span), bf),
            pltpu.VMEM((subs, 16, n * 2 * HALF), bf),
            pltpu.VMEM((subs, 16, n * 2 * HALF), bf),
            dma((2,)), dma((2,)),
            dma((n,)), dma((n,)),
            dma((subs, n)), dma((subs, n)),
            dma((subs, n)), dma((subs, n)),
            dma((subs,)), dma((subs,)),
        ],
        compiler_params=pltpu.CompilerParams(
            collective_id=0, has_side_effects=True, vmem_limit_bytes=56 * 1024 * 1024
        ),
    )(lengths, features, dout, filters, par, tab)


def local(features, dout, filters, taps, skip, lengths):
    blocks = lax.axis_size("seq")
    channels, span = dout.shape
    fits = blocks * span <= DENSE_MAX and taps.shape[1] == 3
    if fits and span % 128 == 0 and channels % (blocks * HALF) == 0:
        return local_kernel(features, dout, filters, taps, skip, lengths)
    return local_general(features, dout, filters, taps, skip, lengths)


def solution(mesh):
    in_specs = (
        P(None, ("chan", "sub"), ("groups", "seq")),
        P(("chan", "sub"), ("groups", "seq")),
        P(("chan", "sub"), "seq"),
        P(None, None, ("chan", "sub")),
        P(("chan", "sub")),
        P("groups"),
    )
    out_specs = (P(("chan", "sub"), ("groups", "seq")), P(None, ("chan", "sub"), ("groups", "seq")))
    return jax.shard_map(local, mesh=mesh, in_specs=in_specs, out_specs=out_specs, check_vma=False)
```

```python
import functools

import jax
import numpy as np
import jax.numpy as jnp
from jax import lax
from jax.experimental import pallas as pl
from jax.experimental.pallas import tpu as pltpu
from jax.sharding import PartitionSpec as P

HIGHEST = lax.Precision.HIGHEST
TWO_PI = 6.283185307179586


def shifted(value, axis, steps):
    count = lax.axis_size(axis)
    leading, last = (max(0, -steps), min(count, count - steps))
    return lax.ppermute(value, axis, [(source, source + steps) for source in range(leading, last)])


def genome_offsets(lengths, positions):
    ends_at = jnp.cumsum(lengths, dtype=jnp.int32)
    before = (ends_at[None, :] <= positions[:, None]).astype(jnp.int32)
    return positions - jnp.sum(before * lengths[None, :], axis=1, dtype=jnp.int32)


def short_forward(extended, taps_local, offsets):
    span_rows = offsets.shape[0]
    count = taps_local.shape[1]
    result = jnp.zeros(extended.shape[:2] + (span_rows,), jnp.float32)
    for tap_index in range(count):
        begin = count - 1 - tap_index
        window = extended[:, :, begin : begin + span_rows].astype(jnp.float32)
        keep_mask = (offsets >= tap_index).astype(jnp.float32)
        result = result + taps_local[:, tap_index, :, None] * window * keep_mask[None, None, :]
    return result


def short_backward(grads_ext, taps_local, offsets_ext):
    count = taps_local.shape[1]
    span_rows = offsets_ext.shape[0] - (count - 1)
    result = jnp.zeros(grads_ext.shape[:2] + (span_rows,), jnp.float32)
    for tap_index in range(count):
        window = grads_ext[:, :, tap_index : tap_index + span_rows]
        keep_mask = (offsets_ext[tap_index : tap_index + span_rows] >= tap_index).astype(
            jnp.float32
        )
        result = result + taps_local[:, tap_index, :, None] * window * keep_mask[None, None, :]
    return result


def dft_table(rows_n, cols_n, period):
    row_ids = jnp.arange(rows_n, dtype=jnp.int32)
    col_ids = jnp.arange(cols_n, dtype=jnp.int32)
    phase = row_ids[:, None] * col_ids[None, :] % period
    angles = phase.astype(jnp.float32) * (-TWO_PI / period)
    return (jnp.cos(angles), jnp.sin(angles))


def forward_transform(signal, tables):
    (row_re, row_im), (twid_re, twid_im), (col_re, col_im) = tables
    half_rows = signal.shape[1] // 128
    blocks_in = signal.reshape(signal.shape[0], half_rows, 128)
    part_re = jnp.einsum("kn,cnm->ckm", row_re[:, :half_rows], blocks_in, precision=HIGHEST)
    part_im = jnp.einsum("kn,cnm->ckm", row_im[:, :half_rows], blocks_in, precision=HIGHEST)
    turned_re = part_re * twid_re - part_im * twid_im
    turned_im = part_re * twid_im + part_im * twid_re
    spec_re = jnp.einsum("ckn,nm->ckm", turned_re, col_re, precision=HIGHEST) - jnp.einsum(
        "ckn,nm->ckm", turned_im, col_im, precision=HIGHEST
    )
    spec_im = jnp.einsum("ckn,nm->ckm", turned_re, col_im, precision=HIGHEST) + jnp.einsum(
        "ckn,nm->ckm", turned_im, col_re, precision=HIGHEST
    )
    return (spec_re, spec_im)


def inverse_transform(spec_re, spec_im, tables):
    (row_re, row_im), (twid_re, twid_im), (col_re, col_im) = tables
    rows_n = spec_re.shape[1]
    half_rows = rows_n // 2
    mid_re = jnp.einsum("ckn,nm->ckm", spec_re, col_re, precision=HIGHEST) + jnp.einsum(
        "ckn,nm->ckm", spec_im, col_im, precision=HIGHEST
    )
    mid_im = jnp.einsum("ckn,nm->ckm", spec_im, col_re, precision=HIGHEST) - jnp.einsum(
        "ckn,nm->ckm", spec_re, col_im, precision=HIGHEST
    )
    back_re = mid_re * twid_re + mid_im * twid_im
    back_im = mid_im * twid_re - mid_re * twid_im
    signal = jnp.einsum("nk,ckm->cnm", row_re[:half_rows], back_re, precision=HIGHEST) + jnp.einsum(
        "nk,ckm->cnm", row_im[:half_rows], back_im, precision=HIGHEST
    )
    return signal.reshape(signal.shape[0], half_rows * 128) * (1.0 / (rows_n * 128))


def long_filter(filt, mixed_in, grad_in, skip_part):
    rows_n = 2 * mixed_in.shape[1] // 128
    tables = (
        dft_table(rows_n, rows_n, rows_n),
        dft_table(rows_n, 128, rows_n * 128),
        dft_table(128, 128, 128),
    )
    mixed_f = mixed_in.astype(jnp.float32)
    grad_f = grad_in.astype(jnp.float32)
    filt_re, filt_im = forward_transform(filt.astype(jnp.float32), tables)
    mix_re, mix_im = forward_transform(mixed_f, tables)
    grad_re, grad_im = forward_transform(grad_f, tables)
    conv_out = inverse_transform(
        filt_re * mix_re - filt_im * mix_im, filt_re * mix_im + filt_im * mix_re, tables
    )
    corr_out = inverse_transform(
        filt_re * grad_re + filt_im * grad_im, filt_re * grad_im - filt_im * grad_re, tables
    )
    y_out = (conv_out + skip_part[:, None] * mixed_f).astype(jnp.bfloat16)
    dmixed = (corr_out + skip_part[:, None] * grad_f).astype(jnp.bfloat16)
    return (y_out, dmixed)


DENSE_MAX = 1024
FINE = 32


def angle_parts(length):
    base = np.arange(length, dtype=np.int64) * 4 + 1
    fine = np.arange(FINE, dtype=np.int64)[:, None] * base[None, :] % (4 * length)
    coarse = np.arange(0, length, FINE, dtype=np.int64)[:, None] * base[None, :] % (4 * length)
    scale = 2.0 * np.pi / (4 * length)
    return [
        func(part * scale).astype(np.float32)
        for part in (coarse, fine)
        for func in (np.cos, np.sin)
    ]


def dense_filter(filt, mixed_in, grad_in, skip_part):
    length = mixed_in.shape[1]
    cc, cs, fc, fs = [jnp.asarray(p)[:, None] if i < 2 else jnp.asarray(p)[None] for i, p in enumerate(angle_parts(length))]
    cos_t = (cc * fc - cs * fs).reshape(length, length)
    sin_t = (cs * fc + cc * fs).reshape(length, length)
    table = jnp.concatenate([cos_t, sin_t], axis=1).astype(jnp.bfloat16)

    def fwd(x):
        return jnp.dot(x, table, preferred_element_type=jnp.float32)

    def inv(x):
        return lax.dot_general(x.astype(jnp.bfloat16), table, (((1,), (1,)), ((), ())), preferred_element_type=jnp.float32) * (1.0 / length)

    h, m, g = fwd(filt), fwd(mixed_in), fwd(grad_in)
    hc, hs = h[:, :length], h[:, length:]
    mc, ms = m[:, :length], m[:, length:]
    gc, gs = g[:, :length], g[:, length:]
    conv_out = inv(jnp.concatenate([hc * mc - hs * ms, hc * ms + hs * mc], axis=1))
    corr_out = inv(jnp.concatenate([hc * gc + hs * gs, hc * gs - hs * gc], axis=1))
    y_out = (conv_out + skip_part[:, None] * mixed_in.astype(jnp.float32)).astype(jnp.bfloat16)
    dmixed = (corr_out + skip_part[:, None] * grad_in.astype(jnp.float32)).astype(jnp.bfloat16)
    return (y_out, dmixed)


def to_channels(stacked):
    return lax.all_to_all(stacked, "seq", split_axis=1, concat_axis=2, tiled=True)


def to_sequence(stacked):
    return lax.all_to_all(stacked, "seq", split_axis=2, concat_axis=1, tiled=True)


def local_general(features, dout, filters, taps, skip, lengths):
    blocks = lax.axis_size("seq")
    seq_rank = lax.axis_index("seq")
    span_rows = features.shape[2]
    channels_here = features.shape[1]
    chan_part = channels_here // blocks
    count = taps.shape[1]
    margin = count - 1
    rim = shifted(features[:, :, span_rows - margin :], "seq", 1)
    extended = jnp.concatenate([rim, features], axis=2)
    first_pos = seq_rank * span_rows
    offsets = genome_offsets(lengths, first_pos + jnp.arange(span_rows, dtype=jnp.int32))
    filtered = short_forward(extended, taps, offsets).astype(jnp.bfloat16)
    query_side = filtered[0].astype(jnp.float32)
    key_side = filtered[1].astype(jnp.float32)
    value_side = filtered[2].astype(jnp.float32)
    dout_f = dout.astype(jnp.float32)
    mixed = (key_side * value_side).astype(jnp.bfloat16)
    grad_in = (dout_f * query_side).astype(jnp.bfloat16)
    moved = to_channels(jnp.stack([mixed, grad_in, filters]))
    skip_part = lax.dynamic_slice_in_dim(skip, seq_rank * chan_part, chan_part, 0)
    run = dense_filter if moved.shape[2] <= DENSE_MAX else long_filter
    y_out, dmixed = run(moved[2], moved[0], moved[1], skip_part)
    returned = to_sequence(jnp.stack([y_out, dmixed]))
    y_here = returned[0].astype(jnp.float32)
    dmixed_here = returned[1].astype(jnp.float32)
    out = (query_side * y_here).astype(jnp.bfloat16)
    grads = jnp.stack([dout_f * y_here, dmixed_here * value_side, dmixed_here * key_side])
    ahead = shifted(grads[:, :, :margin], "seq", -1)
    grads_ext = jnp.concatenate([grads, ahead], axis=2)
    offsets_ext = genome_offsets(
        lengths, first_pos + jnp.arange(span_rows + margin, dtype=jnp.int32)
    )
    dfeatures = short_backward(grads_ext, taps, offsets_ext).astype(jnp.bfloat16)
    return (out, dfeatures)


HALF = 128
NN = (((1,), (0,)), ((), ()))
NT = (((1,), (1,)), ((), ()))
TN = (((0,), (0,)), ((), ()))


def mm(a, b, dims=NN):
    return lax.dot_general(a, b, dims, preferred_element_type=jnp.float32)


def mixer_kernel(
    n,
    lengths_ref, feat_ref, dout_ref, filt_ref, par_ref, tab_ref,
    out_ref, df_ref,
    rim_src, rim, shift_m, place, keep_s, q_s, k_s, v_s, d_s,
    fwd_send, fwd_recv, table, spec, y_send, y_recv, hal_src, hal,
    rim_ss, rim_rs, fwd_ss, fwd_rs, far_ss, far_rs, filt_ss, filt_rs, twin_ss, twin_rs,
    y_ss, y_rs, hal_ss, hal_rs,
):
    rank = lax.axis_index("seq")
    span = feat_ref.shape[2]
    blocks = feat_ref.shape[1] // HALF
    length = span * n
    half = length // 2
    wide = span + 128
    bf = jnp.bfloat16
    f32 = jnp.float32
    group = lax.axis_index("groups")
    side = rank // 2
    inner = (rank == 1) | (rank == 2)
    outer = (rank == 0) | (rank == 3)
    middle = 1 + side
    edge = 3 * side
    across = 2 - side
    near = pl.ds(pl.multiple_of(side * half, 128), half)
    far = pl.ds(pl.multiple_of((1 - side) * half, 128), half)
    mine = pl.ds(pl.multiple_of(rank * span, 128), span)

    def peer(step):
        return lax.rem(rank + 1 + step, n)

    barrier = pltpu.get_barrier_semaphore()
    for step in range(n - 1):
        pl.semaphore_signal(barrier, inc=1, device_id={"seq": peer(step)}, device_id_type=pl.DeviceIdType.MESH)
    pl.semaphore_signal(barrier, inc=1, device_id={"groups": 1 - group}, device_id_type=pl.DeviceIdType.MESH)

    def remote(src, dst, ss, rs, dest):
        return pltpu.make_async_remote_copy(
            src_ref=src, dst_ref=dst, send_sem=ss, recv_sem=rs,
            device_id={"seq": dest}, device_id_type=pl.DeviceIdType.MESH,
        )

    def rim_copy(side, dest):
        return remote(rim_src, rim.at[pl.ds(16 * side, 16)], rim_ss.at[side], rim_rs.at[side], dest)

    def fwd_copy(b):
        return remote(fwd_send.at[b], fwd_recv.at[b, :, mine], fwd_ss.at[b], fwd_rs.at[b], middle)

    def far_copy(b):
        rows = pl.ds(pl.multiple_of(side * HALF, HALF), HALF)
        return remote(fwd_recv.at[b, rows, near], fwd_recv.at[b, rows, near], far_ss.at[b], far_rs.at[b], across)

    def filt_copy(b):
        rows = pl.ds(2 * HALF, HALF)
        return remote(fwd_recv.at[b, rows, near], fwd_recv.at[b, rows, near], filt_ss.at[b], filt_rs.at[b], across)

    def twin_copy(b):
        part = fwd_recv.at[b, pl.ds(2 * HALF, HALF), far]
        return pltpu.make_async_remote_copy(
            src_ref=part, dst_ref=part, send_sem=twin_ss.at[b], recv_sem=twin_rs.at[b],
            device_id={"groups": 1 - group}, device_id_type=pl.DeviceIdType.MESH,
        )

    def y_copy(b):
        return remote(y_send.at[b], y_recv.at[b], y_ss.at[b], y_rs.at[b], edge)

    def hal_copy(b, dest):
        return remote(hal_src.at[b], hal.at[b], hal_ss.at[b], hal_rs.at[b], dest)

    r_id = lax.broadcasted_iota(jnp.int32, (16, span), 0)
    p_id = lax.broadcasted_iota(jnp.int32, (16, span), 1)
    total = None
    for a in range(4):
        hit = (
            ((r_id == 4 * a) & (p_id == span - 2)) | ((r_id == 4 * a + 1) & (p_id == span - 1))
            | ((r_id == 4 * a + 2) & (p_id == 0)) | ((r_id == 4 * a + 3) & (p_id == 1))
        )
        pick = jnp.where(hit, 1.0, 0.0).astype(bf)
        term = mm(pick, feat_ref[a] if a < 3 else dout_ref[...], NT)
        total = term if total is None else total + term
    rim_src[...] = total.astype(bf)

    @pl.when(rank == 0)
    def _():
        rim[0:16, :] = jnp.zeros((16, rim.shape[1]), bf)

    @pl.when(rank == n - 1)
    def _():
        rim[16:32, :] = jnp.zeros((16, rim.shape[1]), bf)
        hal[...] = jnp.zeros(hal.shape, bf)

    @pl.when(inner)
    def _():
        rows = pl.ds(pl.multiple_of(side * HALF, HALF), HALF)
        for b in range(blocks):
            fwd_recv[b, rows, far] = jnp.zeros((HALF, half), bf)

    pl.semaphore_wait(barrier, n)

    @pl.when(rank < n - 1)
    def _():
        rim_copy(0, rank + 1).start()

    @pl.when(rank > 0)
    def _():
        rim_copy(1, rank - 1).start()

    def offsets_of(ahead, width):
        position = rank * span + ahead + lax.broadcasted_iota(jnp.int32, (8, width), 1)
        result = position
        end = jnp.int32(0)
        for g in range(lengths_ref.shape[0]):
            one = lengths_ref[g]
            end = end + one
            result = result - jnp.where(end <= position, one, 0)
        return result

    off_wide = offsets_of(0, wide)
    keep_s[0] = jnp.where(offsets_of(1, span) >= 1, 1.0, 0.0)
    keep_s[1] = jnp.where(offsets_of(2, span) >= 2, 1.0, 0.0)
    src_id = lax.broadcasted_iota(jnp.int32, (span, wide), 0)
    dst_id = lax.broadcasted_iota(jnp.int32, (span, wide), 1)
    row_id = lax.broadcasted_iota(jnp.int32, (32, wide), 0)
    col_id = lax.broadcasted_iota(jnp.int32, (32, wide), 1)
    for j in range(3):
        keep = jnp.where(off_wide >= j, 1.0, 0.0)[0:1, :]
        shift_m[j] = (jnp.where(dst_id - j == src_id, 1.0, 0.0) * keep).astype(bf)
        for a in range(4):
            hit = (
                ((row_id == 4 * a) & (col_id - j == -2)) | ((row_id == 4 * a + 1) & (col_id - j == -1))
                | ((row_id == 16 + 4 * a + 2) & (col_id - j == span))
                | ((row_id == 16 + 4 * a + 3) & (col_id - j == span + 1))
            )
            place[a, j] = (jnp.where(hit, 1.0, 0.0) * keep).astype(bf)

    @pl.when(rank > 0)
    def _():
        rim_copy(0, rank).wait_recv()

    @pl.when(rank < n - 1)
    def _():
        rim_copy(1, rank).wait_recv()

    def prepare(b):
        rows = pl.ds(pl.multiple_of(b * HALF, HALF), HALF)
        rim_part = rim[:, rows]
        par = par_ref[rows, :]

        def shifted_in(a, j):
            source = feat_ref[a, rows, :] if a < 3 else dout_ref[rows, :]
            return mm(source, shift_m[j]) + mm(rim_part, place[a, j], TN)

        result = []
        for a in range(3):
            acc = par[:, 3 * a : 3 * a + 1] * shifted_in(a, 0)
            acc = acc + par[:, 3 * a + 1 : 3 * a + 2] * shifted_in(a, 1)
            acc = acc + par[:, 3 * a + 2 : 3 * a + 3] * shifted_in(a, 2)
            result.append(acc.astype(bf))
        d_wide = shifted_in(3, 0).astype(bf)
        q_s[rows, :] = result[0][:, :span]
        k_s[rows, :] = result[1]
        v_s[rows, :] = result[2]
        d_s[rows, :] = d_wide
        mixed = (result[1][:, :span].astype(f32) * result[2][:, :span].astype(f32)).astype(bf)
        grad_in = (d_wide[:, :span].astype(f32) * result[0][:, :span].astype(f32)).astype(bf)

        @pl.when(outer)
        def _():
            fwd_send[b, 0:HALF, :] = mixed
            fwd_send[b, HALF : 2 * HALF, :] = grad_in
            fwd_send[b, 2 * HALF :, :] = filt_ref[rows, :]
            fwd_copy(b).start()

        @pl.when(inner)
        def _():
            fwd_recv[b, 0:HALF, mine] = mixed
            fwd_recv[b, HALF : 2 * HALF, mine] = grad_in
            fwd_recv[b, 2 * HALF :, mine] = filt_ref[rows, :]

    def own(b):
        return lax.rem(b, 2) == group

    def relay(b):
        fwd_copy(b).wait_recv()
        far_copy(b).start()

        @pl.when(own(b))
        def _():
            filt_copy(b).start()

    def collect(b):
        far_copy(b).wait_recv()

        @pl.when(own(b))
        def _():
            filt_copy(b).wait_recv()
            twin_copy(b).start()

    fine_c = tab_ref[2]
    fine_s = tab_ref[3]

    def build(a, carry):
        big_c = tab_ref[0, pl.ds(a, 1), :]
        big_s = tab_ref[1, pl.ds(a, 1), :]
        rows = pl.ds(pl.multiple_of(a * FINE, FINE), FINE)
        table[rows, 0:length] = (big_c * fine_c - big_s * fine_s).astype(bf)
        table[rows, length:] = (big_s * fine_c + big_c * fine_s).astype(bf)
        return carry

    tile = 256

    def transform(b):
        @pl.when(jnp.logical_not(own(b)))
        def _():
            twin_copy(b).wait_recv()

        def spectrum_tile(t, carry):
            cols = pl.ds(pl.multiple_of(t * tile, tile), tile)
            sins = pl.ds(pl.multiple_of(length + t * tile, tile), tile)
            signal = fwd_recv[b]
            x_c = mm(signal, table[:, cols])
            x_s = mm(signal, table[:, sins])
            h_c = x_c[2 * HALF :]
            h_s = x_s[2 * HALF :]
            m_c, g_c = x_c[:HALF], x_c[HALF : 2 * HALF]
            m_s, g_s = x_s[:HALF], x_s[HALF : 2 * HALF]
            spec[0:HALF, cols] = (h_c * m_c - h_s * m_s).astype(bf)
            spec[0:HALF, sins] = (h_c * m_s + h_s * m_c).astype(bf)
            spec[HALF:, cols] = (h_c * g_c + h_s * g_s).astype(bf)
            spec[HALF:, sins] = (h_c * g_s - h_s * g_c).astype(bf)
            return carry

        lax.fori_loop(0, length // tile, spectrum_tile, 0)
        skip_col = par_ref[pl.ds(pl.multiple_of(b * HALF, HALF), HALF), 9:10]

        def results(dest):
            cols = pl.ds(pl.multiple_of(dest * span, 128), span)
            value = mm(spec[...], table[cols, :], NT) * (1.0 / length)
            signal = fwd_recv[b, 0 : 2 * HALF, cols].astype(f32)
            y_part = (value[:HALF] + skip_col * signal[:HALF]).astype(bf)
            d_part = (value[HALF:] + skip_col * signal[HALF:]).astype(bf)
            return y_part, d_part

        y_part, d_part = results(edge)
        y_send[b, 0:HALF, :] = y_part
        y_send[b, HALF:, :] = d_part
        y_copy(b).start()
        y_part, d_part = results(rank)
        y_recv[b, 0:HALF, :] = y_part
        y_recv[b, HALF:, :] = d_part

    r_id = lax.broadcasted_iota(jnp.int32, (16, 128), 0)
    c_id = lax.broadcasted_iota(jnp.int32, (16, 128), 1)
    eye = jnp.where((r_id == c_id) & (r_id < 2), 1.0, 0.0).astype(bf)

    def halo_send(b):
        @pl.when(outer)
        def _():
            y_copy(b).wait_recv()

        hal_src[b] = mm(eye, y_recv[b, :, 0:128], NT).astype(bf)

        @pl.when(rank > 0)
        def _():
            hal_copy(b, rank - 1).start()

    def finish(b):
        @pl.when(rank < n - 1)
        def _():
            hal_copy(b, rank).wait_recv()

        if True:
            rows = pl.ds(pl.multiple_of(b * HALF, HALF), HALF)
            par = par_ref[rows, :]
            y_rim = mm(hal[b, :, 0:HALF], eye, TN)
            d_rim = mm(hal[b, :, HALF:], eye, TN)
            y_here = y_recv[b, 0:HALF, :].astype(f32)
            d_here = y_recv[b, HALF:, :].astype(f32)
            out_ref[rows, :] = (q_s[rows, :].astype(f32) * y_here).astype(bf)
            y_wide = jnp.concatenate([y_here, y_rim], axis=1)
            d_wide = jnp.concatenate([d_here, d_rim], axis=1)
            for c in range(3):
                if c == 0:
                    grads = d_s[rows, :].astype(f32) * y_wide
                elif c == 1:
                    grads = d_wide * v_s[rows, :].astype(f32)
                else:
                    grads = d_wide * k_s[rows, :].astype(f32)
                acc = par[:, 3 * c : 3 * c + 1] * grads[:, :span]
                for j in (1, 2):
                    moved = pltpu.roll(grads, wide - j, 1)[:, :span]
                    acc = acc + par[:, 3 * c + j : 3 * c + j + 1] * moved * keep_s[j - 1, 0:1, :]
                df_ref[c, rows, :] = acc.astype(bf)

    def at(step, lag, work, only=None):
        b = step - lag
        ready = (b >= 0) & (b < blocks)

        @pl.when(ready if only is None else ready & only)
        def _():
            work(b)

    def advance(step, carry):
        at(step, 0, prepare)
        at(step, 1, relay, inner)
        at(step, 4, collect, inner)
        at(step, 5, transform, inner)
        at(step, 6, halo_send)
        at(step, 7, finish)

        @pl.when(step == 2)
        def _():
            lax.fori_loop(0, length // FINE, build, 0)

        return carry

    lax.fori_loop(0, blocks + 7, advance, 0)

    @pl.when(rank < n - 1)
    def _():
        rim_copy(0, rank).wait_send()

    @pl.when(rank > 0)
    def _():
        rim_copy(1, rank).wait_send()

    def drain(b, carry):
        @pl.when(rank > 0)
        def _():
            hal_copy(b, rank).wait_send()

        @pl.when(outer)
        def _():
            fwd_copy(b).wait_send()

        @pl.when(inner)
        def _():
            far_copy(b).wait_send()
            y_copy(b).wait_send()

        @pl.when(inner & own(b))
        def _():
            filt_copy(b).wait_send()
            twin_copy(b).wait_send()

        return carry

    lax.fori_loop(0, blocks, drain, 0)


def local_kernel(features, dout, filters, taps, skip, lengths):
    n = lax.axis_size("seq")
    channels, span = dout.shape
    blocks = channels // HALF
    length = n * span
    wide = span + 128
    bf = jnp.bfloat16
    par = jnp.concatenate([taps.reshape(9, channels), skip[None]], axis=0).T
    tab = jnp.asarray(np.stack(angle_parts(length)))
    vmem = pl.BlockSpec(memory_space=pltpu.VMEM)
    dma = pltpu.SemaphoreType.DMA
    return pl.pallas_call(
        functools.partial(mixer_kernel, n),
        out_shape=(
            jax.ShapeDtypeStruct(dout.shape, bf),
            jax.ShapeDtypeStruct(features.shape, bf),
        ),
        in_specs=[pl.BlockSpec(memory_space=pltpu.SMEM)] + [vmem] * 5,
        out_specs=(vmem, vmem),
        scratch_shapes=[
            pltpu.VMEM((16, channels), bf),
            pltpu.VMEM((32, channels), bf),
            pltpu.VMEM((3, span, wide), bf),
            pltpu.VMEM((4, 3, 32, wide), bf),
            pltpu.VMEM((2, 8, span), jnp.float32),
            pltpu.VMEM((channels, span), bf),
            pltpu.VMEM((channels, wide), bf),
            pltpu.VMEM((channels, wide), bf),
            pltpu.VMEM((channels, wide), bf),
            pltpu.VMEM((blocks, 3 * HALF, span), bf),
            pltpu.VMEM((blocks, 3 * HALF, length), bf),
            pltpu.VMEM((length, 2 * length), bf),
            pltpu.VMEM((2 * HALF, 2 * length), bf),
            pltpu.VMEM((blocks, 2 * HALF, span), bf),
            pltpu.VMEM((blocks, 2 * HALF, span), bf),
            pltpu.VMEM((blocks, 16, 2 * HALF), bf),
            pltpu.VMEM((blocks, 16, 2 * HALF), bf),
            dma((2,)), dma((2,)),
            dma((blocks,)), dma((blocks,)),
            dma((blocks,)), dma((blocks,)),
            dma((blocks,)), dma((blocks,)),
            dma((blocks,)), dma((blocks,)),
            dma((blocks,)), dma((blocks,)),
            dma((blocks,)), dma((blocks,)),
        ],
        compiler_params=pltpu.CompilerParams(
            collective_id=0, has_side_effects=True, vmem_limit_bytes=56 * 1024 * 1024
        ),
    )(lengths, features, dout, filters, par, tab)


def local(features, dout, filters, taps, skip, lengths):
    blocks = lax.axis_size("seq")
    channels, span = dout.shape
    fits = blocks == 4 and lax.axis_size("groups") == 2 and blocks * span <= DENSE_MAX and taps.shape[1] == 3
    if fits and span % 128 == 0 and channels % HALF == 0:
        return local_kernel(features, dout, filters, taps, skip, lengths)
    return local_general(features, dout, filters, taps, skip, lengths)


def solution(mesh):
    in_specs = (
        P(None, ("chan", "sub"), ("groups", "seq")),
        P(("chan", "sub"), ("groups", "seq")),
        P(("chan", "sub"), "seq"),
        P(None, None, ("chan", "sub")),
        P(("chan", "sub")),
        P("groups"),
    )
    out_specs = (P(("chan", "sub"), ("groups", "seq")), P(None, ("chan", "sub"), ("groups", "seq")))
    return jax.shard_map(local, mesh=mesh, in_specs=in_specs, out_specs=out_specs, check_vma=False)
```

```python
import functools

import jax
import numpy as np
import jax.numpy as jnp
from jax import lax
from jax.experimental import pallas as pl
from jax.experimental.pallas import tpu as pltpu
from jax.sharding import PartitionSpec as P

HIGHEST = lax.Precision.HIGHEST
TWO_PI = 6.283185307179586


def shifted(value, axis, steps):
    count = lax.axis_size(axis)
    leading, last = (max(0, -steps), min(count, count - steps))
    return lax.ppermute(value, axis, [(source, source + steps) for source in range(leading, last)])


def genome_offsets(lengths, positions):
    ends_at = jnp.cumsum(lengths, dtype=jnp.int32)
    before = (ends_at[None, :] <= positions[:, None]).astype(jnp.int32)
    return positions - jnp.sum(before * lengths[None, :], axis=1, dtype=jnp.int32)


def short_forward(extended, taps_local, offsets):
    span_rows = offsets.shape[0]
    count = taps_local.shape[1]
    result = jnp.zeros(extended.shape[:2] + (span_rows,), jnp.float32)
    for tap_index in range(count):
        begin = count - 1 - tap_index
        window = extended[:, :, begin : begin + span_rows].astype(jnp.float32)
        keep_mask = (offsets >= tap_index).astype(jnp.float32)
        result = result + taps_local[:, tap_index, :, None] * window * keep_mask[None, None, :]
    return result


def short_backward(grads_ext, taps_local, offsets_ext):
    count = taps_local.shape[1]
    span_rows = offsets_ext.shape[0] - (count - 1)
    result = jnp.zeros(grads_ext.shape[:2] + (span_rows,), jnp.float32)
    for tap_index in range(count):
        window = grads_ext[:, :, tap_index : tap_index + span_rows]
        keep_mask = (offsets_ext[tap_index : tap_index + span_rows] >= tap_index).astype(
            jnp.float32
        )
        result = result + taps_local[:, tap_index, :, None] * window * keep_mask[None, None, :]
    return result


def dft_table(rows_n, cols_n, period):
    row_ids = jnp.arange(rows_n, dtype=jnp.int32)
    col_ids = jnp.arange(cols_n, dtype=jnp.int32)
    phase = row_ids[:, None] * col_ids[None, :] % period
    angles = phase.astype(jnp.float32) * (-TWO_PI / period)
    return (jnp.cos(angles), jnp.sin(angles))


def forward_transform(signal, tables):
    (row_re, row_im), (twid_re, twid_im), (col_re, col_im) = tables
    half_rows = signal.shape[1] // 128
    blocks_in = signal.reshape(signal.shape[0], half_rows, 128)
    part_re = jnp.einsum("kn,cnm->ckm", row_re[:, :half_rows], blocks_in, precision=HIGHEST)
    part_im = jnp.einsum("kn,cnm->ckm", row_im[:, :half_rows], blocks_in, precision=HIGHEST)
    turned_re = part_re * twid_re - part_im * twid_im
    turned_im = part_re * twid_im + part_im * twid_re
    spec_re = jnp.einsum("ckn,nm->ckm", turned_re, col_re, precision=HIGHEST) - jnp.einsum(
        "ckn,nm->ckm", turned_im, col_im, precision=HIGHEST
    )
    spec_im = jnp.einsum("ckn,nm->ckm", turned_re, col_im, precision=HIGHEST) + jnp.einsum(
        "ckn,nm->ckm", turned_im, col_re, precision=HIGHEST
    )
    return (spec_re, spec_im)


def inverse_transform(spec_re, spec_im, tables):
    (row_re, row_im), (twid_re, twid_im), (col_re, col_im) = tables
    rows_n = spec_re.shape[1]
    half_rows = rows_n // 2
    mid_re = jnp.einsum("ckn,nm->ckm", spec_re, col_re, precision=HIGHEST) + jnp.einsum(
        "ckn,nm->ckm", spec_im, col_im, precision=HIGHEST
    )
    mid_im = jnp.einsum("ckn,nm->ckm", spec_im, col_re, precision=HIGHEST) - jnp.einsum(
        "ckn,nm->ckm", spec_re, col_im, precision=HIGHEST
    )
    back_re = mid_re * twid_re + mid_im * twid_im
    back_im = mid_im * twid_re - mid_re * twid_im
    signal = jnp.einsum("nk,ckm->cnm", row_re[:half_rows], back_re, precision=HIGHEST) + jnp.einsum(
        "nk,ckm->cnm", row_im[:half_rows], back_im, precision=HIGHEST
    )
    return signal.reshape(signal.shape[0], half_rows * 128) * (1.0 / (rows_n * 128))


def long_filter(filt, mixed_in, grad_in, skip_part):
    rows_n = 2 * mixed_in.shape[1] // 128
    tables = (
        dft_table(rows_n, rows_n, rows_n),
        dft_table(rows_n, 128, rows_n * 128),
        dft_table(128, 128, 128),
    )
    mixed_f = mixed_in.astype(jnp.float32)
    grad_f = grad_in.astype(jnp.float32)
    filt_re, filt_im = forward_transform(filt.astype(jnp.float32), tables)
    mix_re, mix_im = forward_transform(mixed_f, tables)
    grad_re, grad_im = forward_transform(grad_f, tables)
    conv_out = inverse_transform(
        filt_re * mix_re - filt_im * mix_im, filt_re * mix_im + filt_im * mix_re, tables
    )
    corr_out = inverse_transform(
        filt_re * grad_re + filt_im * grad_im, filt_re * grad_im - filt_im * grad_re, tables
    )
    y_out = (conv_out + skip_part[:, None] * mixed_f).astype(jnp.bfloat16)
    dmixed = (corr_out + skip_part[:, None] * grad_f).astype(jnp.bfloat16)
    return (y_out, dmixed)


DENSE_MAX = 1024
FINE = 32


def angle_parts(length):
    base = np.arange(length, dtype=np.int64) * 4 + 1
    fine = np.arange(FINE, dtype=np.int64)[:, None] * base[None, :] % (4 * length)
    coarse = np.arange(0, length, FINE, dtype=np.int64)[:, None] * base[None, :] % (4 * length)
    scale = 2.0 * np.pi / (4 * length)
    return [
        func(part * scale).astype(np.float32)
        for part in (coarse, fine)
        for func in (np.cos, np.sin)
    ]


def dense_filter(filt, mixed_in, grad_in, skip_part):
    length = mixed_in.shape[1]
    cc, cs, fc, fs = [jnp.asarray(p)[:, None] if i < 2 else jnp.asarray(p)[None] for i, p in enumerate(angle_parts(length))]
    cos_t = (cc * fc - cs * fs).reshape(length, length)
    sin_t = (cs * fc + cc * fs).reshape(length, length)
    table = jnp.concatenate([cos_t, sin_t], axis=1).astype(jnp.bfloat16)

    def fwd(x):
        return jnp.dot(x, table, preferred_element_type=jnp.float32)

    def inv(x):
        return lax.dot_general(x.astype(jnp.bfloat16), table, (((1,), (1,)), ((), ())), preferred_element_type=jnp.float32) * (1.0 / length)

    h, m, g = fwd(filt), fwd(mixed_in), fwd(grad_in)
    hc, hs = h[:, :length], h[:, length:]
    mc, ms = m[:, :length], m[:, length:]
    gc, gs = g[:, :length], g[:, length:]
    conv_out = inv(jnp.concatenate([hc * mc - hs * ms, hc * ms + hs * mc], axis=1))
    corr_out = inv(jnp.concatenate([hc * gc + hs * gs, hc * gs - hs * gc], axis=1))
    y_out = (conv_out + skip_part[:, None] * mixed_in.astype(jnp.float32)).astype(jnp.bfloat16)
    dmixed = (corr_out + skip_part[:, None] * grad_in.astype(jnp.float32)).astype(jnp.bfloat16)
    return (y_out, dmixed)


def to_channels(stacked):
    return lax.all_to_all(stacked, "seq", split_axis=1, concat_axis=2, tiled=True)


def to_sequence(stacked):
    return lax.all_to_all(stacked, "seq", split_axis=2, concat_axis=1, tiled=True)


def local_general(features, dout, filters, taps, skip, lengths):
    blocks = lax.axis_size("seq")
    seq_rank = lax.axis_index("seq")
    span_rows = features.shape[2]
    channels_here = features.shape[1]
    chan_part = channels_here // blocks
    count = taps.shape[1]
    margin = count - 1
    rim = shifted(features[:, :, span_rows - margin :], "seq", 1)
    extended = jnp.concatenate([rim, features], axis=2)
    first_pos = seq_rank * span_rows
    offsets = genome_offsets(lengths, first_pos + jnp.arange(span_rows, dtype=jnp.int32))
    filtered = short_forward(extended, taps, offsets).astype(jnp.bfloat16)
    query_side = filtered[0].astype(jnp.float32)
    key_side = filtered[1].astype(jnp.float32)
    value_side = filtered[2].astype(jnp.float32)
    dout_f = dout.astype(jnp.float32)
    mixed = (key_side * value_side).astype(jnp.bfloat16)
    grad_in = (dout_f * query_side).astype(jnp.bfloat16)
    moved = to_channels(jnp.stack([mixed, grad_in, filters]))
    skip_part = lax.dynamic_slice_in_dim(skip, seq_rank * chan_part, chan_part, 0)
    run = dense_filter if moved.shape[2] <= DENSE_MAX else long_filter
    y_out, dmixed = run(moved[2], moved[0], moved[1], skip_part)
    returned = to_sequence(jnp.stack([y_out, dmixed]))
    y_here = returned[0].astype(jnp.float32)
    dmixed_here = returned[1].astype(jnp.float32)
    out = (query_side * y_here).astype(jnp.bfloat16)
    grads = jnp.stack([dout_f * y_here, dmixed_here * value_side, dmixed_here * key_side])
    ahead = shifted(grads[:, :, :margin], "seq", -1)
    grads_ext = jnp.concatenate([grads, ahead], axis=2)
    offsets_ext = genome_offsets(
        lengths, first_pos + jnp.arange(span_rows + margin, dtype=jnp.int32)
    )
    dfeatures = short_backward(grads_ext, taps, offsets_ext).astype(jnp.bfloat16)
    return (out, dfeatures)


HALF = 128
NN = (((1,), (0,)), ((), ()))
NT = (((1,), (1,)), ((), ()))
TN = (((0,), (0,)), ((), ()))


def mm(a, b, dims=NN):
    return lax.dot_general(a, b, dims, preferred_element_type=jnp.float32)


def mixer_kernel(
    n,
    lengths_ref, feat_ref, dout_ref, filt_ref, par_ref, tab_ref,
    out_ref, df_ref,
    rim_src, rim, shift_m, place, keep_s, q_s, k_s, v_s, d_s,
    fwd_send, fwd_recv, table, spec, y_send, y_recv, hal_src, hal,
    rim_ss, rim_rs, fwd_ss, fwd_rs, far_ss, far_rs, filt_ss, filt_rs, twin_ss, twin_rs,
    y_ss, y_rs, hal_ss, hal_rs,
):
    rank = lax.axis_index("seq")
    span = feat_ref.shape[2]
    blocks = feat_ref.shape[1] // HALF
    length = span * n
    half = length // 2
    wide = span + 128
    bf = jnp.bfloat16
    f32 = jnp.float32
    group = lax.axis_index("groups")
    side = rank // 2
    inner = (rank == 1) | (rank == 2)
    outer = (rank == 0) | (rank == 3)
    middle = 1 + side
    edge = 3 * side
    across = 2 - side
    near = pl.ds(pl.multiple_of(side * half, 128), half)
    far = pl.ds(pl.multiple_of((1 - side) * half, 128), half)
    mine = pl.ds(pl.multiple_of(rank * span, 128), span)

    def peer(step):
        return lax.rem(rank + 1 + step, n)

    barrier = pltpu.get_barrier_semaphore()
    for step in range(n - 1):
        pl.semaphore_signal(barrier, inc=1, device_id={"seq": peer(step)}, device_id_type=pl.DeviceIdType.MESH)
    pl.semaphore_signal(barrier, inc=1, device_id={"groups": 1 - group}, device_id_type=pl.DeviceIdType.MESH)

    def remote(src, dst, ss, rs, dest):
        return pltpu.make_async_remote_copy(
            src_ref=src, dst_ref=dst, send_sem=ss, recv_sem=rs,
            device_id={"seq": dest}, device_id_type=pl.DeviceIdType.MESH,
        )

    def rim_copy(side, dest):
        return remote(rim_src, rim.at[pl.ds(16 * side, 16)], rim_ss.at[side], rim_rs.at[side], dest)

    def fwd_copy(b):
        return remote(fwd_send.at[b], fwd_recv.at[b, :, mine], fwd_ss.at[b], fwd_rs.at[b], middle)

    def far_copy(b):
        rows = pl.ds(pl.multiple_of(side * HALF, HALF), HALF)
        return remote(fwd_recv.at[b, rows, near], fwd_recv.at[b, rows, near], far_ss.at[b], far_rs.at[b], across)

    def filt_copy(b):
        rows = pl.ds(2 * HALF, HALF)
        return remote(fwd_recv.at[b, rows, near], fwd_recv.at[b, rows, near], filt_ss.at[b], filt_rs.at[b], across)

    def twin_copy(b):
        part = fwd_recv.at[b, pl.ds(2 * HALF, HALF), far]
        return pltpu.make_async_remote_copy(
            src_ref=part, dst_ref=part, send_sem=twin_ss.at[b], recv_sem=twin_rs.at[b],
            device_id={"groups": 1 - group}, device_id_type=pl.DeviceIdType.MESH,
        )

    def y_copy(b):
        return remote(y_send.at[b], y_recv.at[b], y_ss.at[b], y_rs.at[b], edge)

    def hal_copy(b, dest):
        return remote(hal_src.at[b], hal.at[b], hal_ss.at[b], hal_rs.at[b], dest)

    r_id = lax.broadcasted_iota(jnp.int32, (16, span), 0)
    p_id = lax.broadcasted_iota(jnp.int32, (16, span), 1)
    total = None
    for a in range(4):
        hit = (
            ((r_id == 4 * a) & (p_id == span - 2)) | ((r_id == 4 * a + 1) & (p_id == span - 1))
            | ((r_id == 4 * a + 2) & (p_id == 0)) | ((r_id == 4 * a + 3) & (p_id == 1))
        )
        pick = jnp.where(hit, 1.0, 0.0).astype(bf)
        term = mm(pick, feat_ref[a] if a < 3 else dout_ref[...], NT)
        total = term if total is None else total + term
    rim_src[...] = total.astype(bf)

    @pl.when(rank == 0)
    def _():
        rim[0:16, :] = jnp.zeros((16, rim.shape[1]), bf)

    @pl.when(rank == n - 1)
    def _():
        rim[16:32, :] = jnp.zeros((16, rim.shape[1]), bf)
        hal[...] = jnp.zeros(hal.shape, bf)

    @pl.when(inner)
    def _():
        rows = pl.ds(pl.multiple_of(side * HALF, HALF), HALF)
        for b in range(blocks):
            fwd_recv[b, rows, far] = jnp.zeros((HALF, half), bf)

    pl.semaphore_wait(barrier, n)

    @pl.when(rank < n - 1)
    def _():
        rim_copy(0, rank + 1).start()

    @pl.when(rank > 0)
    def _():
        rim_copy(1, rank - 1).start()

    def offsets_of(ahead, width):
        position = rank * span + ahead + lax.broadcasted_iota(jnp.int32, (8, width), 1)
        result = position
        end = jnp.int32(0)
        for g in range(lengths_ref.shape[0]):
            one = lengths_ref[g]
            end = end + one
            result = result - jnp.where(end <= position, one, 0)
        return result

    off_wide = offsets_of(0, wide)
    keep_s[0] = jnp.where(offsets_of(1, span) >= 1, 1.0, 0.0)
    keep_s[1] = jnp.where(offsets_of(2, span) >= 2, 1.0, 0.0)
    src_id = lax.broadcasted_iota(jnp.int32, (span, wide), 0)
    dst_id = lax.broadcasted_iota(jnp.int32, (span, wide), 1)
    row_id = lax.broadcasted_iota(jnp.int32, (32, wide), 0)
    col_id = lax.broadcasted_iota(jnp.int32, (32, wide), 1)
    for j in range(3):
        keep = jnp.where(off_wide >= j, 1.0, 0.0)[0:1, :]
        shift_m[j] = (jnp.where(dst_id - j == src_id, 1.0, 0.0) * keep).astype(bf)
        for a in range(4):
            hit = (
                ((row_id == 4 * a) & (col_id - j == -2)) | ((row_id == 4 * a + 1) & (col_id - j == -1))
                | ((row_id == 16 + 4 * a + 2) & (col_id - j == span))
                | ((row_id == 16 + 4 * a + 3) & (col_id - j == span + 1))
            )
            place[a, j] = (jnp.where(hit, 1.0, 0.0) * keep).astype(bf)

    @pl.when(rank > 0)
    def _():
        rim_copy(0, rank).wait_recv()

    @pl.when(rank < n - 1)
    def _():
        rim_copy(1, rank).wait_recv()

    def prepare(b):
        rows = pl.ds(pl.multiple_of(b * HALF, HALF), HALF)
        rim_part = rim[:, rows]
        par = par_ref[rows, :]

        def shifted_in(a, j):
            source = feat_ref[a, rows, :] if a < 3 else dout_ref[rows, :]
            return mm(source, shift_m[j]) + mm(rim_part, place[a, j], TN)

        result = []
        for a in range(3):
            acc = par[:, 3 * a : 3 * a + 1] * shifted_in(a, 0)
            acc = acc + par[:, 3 * a + 1 : 3 * a + 2] * shifted_in(a, 1)
            acc = acc + par[:, 3 * a + 2 : 3 * a + 3] * shifted_in(a, 2)
            result.append(acc.astype(bf))
        d_wide = shifted_in(3, 0).astype(bf)
        q_s[rows, :] = result[0][:, :span]
        k_s[rows, :] = result[1]
        v_s[rows, :] = result[2]
        d_s[rows, :] = d_wide
        mixed = (result[1][:, :span].astype(f32) * result[2][:, :span].astype(f32)).astype(bf)
        grad_in = (d_wide[:, :span].astype(f32) * result[0][:, :span].astype(f32)).astype(bf)

        @pl.when(outer)
        def _():
            fwd_send[b, 0:HALF, :] = mixed
            fwd_send[b, HALF : 2 * HALF, :] = grad_in
            fwd_send[b, 2 * HALF :, :] = filt_ref[rows, :]
            fwd_copy(b).start()

        @pl.when(inner)
        def _():
            fwd_recv[b, 0:HALF, mine] = mixed
            fwd_recv[b, HALF : 2 * HALF, mine] = grad_in
            fwd_recv[b, 2 * HALF :, mine] = filt_ref[rows, :]

    def own(b):
        return lax.rem(b, 2) == group

    def relay(b):
        fwd_copy(b).wait_recv()
        far_copy(b).start()

        @pl.when(own(b))
        def _():
            filt_copy(b).start()

    def collect(b):
        far_copy(b).wait_recv()

        @pl.when(own(b))
        def _():
            filt_copy(b).wait_recv()
            twin_copy(b).start()

    fine_c = tab_ref[2]
    fine_s = tab_ref[3]

    def build(a, carry):
        big_c = tab_ref[0, pl.ds(a, 1), :]
        big_s = tab_ref[1, pl.ds(a, 1), :]
        rows = pl.ds(pl.multiple_of(a * FINE, FINE), FINE)
        table[rows, 0:length] = (big_c * fine_c - big_s * fine_s).astype(bf)
        table[rows, length:] = (big_s * fine_c + big_c * fine_s).astype(bf)
        return carry

    tile = 256

    def transform(b):
        @pl.when(jnp.logical_not(own(b)))
        def _():
            twin_copy(b).wait_recv()

        def spectrum_tile(t, carry):
            cols = pl.ds(pl.multiple_of(t * tile, tile), tile)
            sins = pl.ds(pl.multiple_of(length + t * tile, tile), tile)
            signal = fwd_recv[b]
            x_c = mm(signal, table[:, cols])
            x_s = mm(signal, table[:, sins])
            h_c = x_c[2 * HALF :]
            h_s = x_s[2 * HALF :]
            m_c, g_c = x_c[:HALF], x_c[HALF : 2 * HALF]
            m_s, g_s = x_s[:HALF], x_s[HALF : 2 * HALF]
            spec[0:HALF, cols] = (h_c * m_c - h_s * m_s).astype(bf)
            spec[0:HALF, sins] = (h_c * m_s + h_s * m_c).astype(bf)
            spec[HALF:, cols] = (h_c * g_c + h_s * g_s).astype(bf)
            spec[HALF:, sins] = (h_c * g_s - h_s * g_c).astype(bf)
            return carry

        lax.fori_loop(0, length // tile, spectrum_tile, 0)
        skip_col = par_ref[pl.ds(pl.multiple_of(b * HALF, HALF), HALF), 9:10]

        def results(dest):
            cols = pl.ds(pl.multiple_of(dest * span, 128), span)
            value = mm(spec[...], table[cols, :], NT) * (1.0 / length)
            signal = fwd_recv[b, 0 : 2 * HALF, cols].astype(f32)
            y_part = (value[:HALF] + skip_col * signal[:HALF]).astype(bf)
            d_part = (value[HALF:] + skip_col * signal[HALF:]).astype(bf)
            return y_part, d_part

        y_part, d_part = results(edge)
        y_send[b, 0:HALF, :] = y_part
        y_send[b, HALF:, :] = d_part
        y_copy(b).start()
        y_part, d_part = results(rank)
        y_recv[b, 0:HALF, :] = y_part
        y_recv[b, HALF:, :] = d_part

    r_id = lax.broadcasted_iota(jnp.int32, (16, 128), 0)
    c_id = lax.broadcasted_iota(jnp.int32, (16, 128), 1)
    eye = jnp.where((r_id == c_id) & (r_id < 2), 1.0, 0.0).astype(bf)

    def halo_send(b):
        @pl.when(outer)
        def _():
            y_copy(b).wait_recv()

        hal_src[b] = mm(eye, y_recv[b, :, 0:128], NT).astype(bf)

        @pl.when(rank > 0)
        def _():
            hal_copy(b, rank - 1).start()

    def finish(b):
        @pl.when(rank < n - 1)
        def _():
            hal_copy(b, rank).wait_recv()

        if True:
            rows = pl.ds(pl.multiple_of(b * HALF, HALF), HALF)
            par = par_ref[rows, :]
            y_rim = mm(hal[b, :, 0:HALF], eye, TN)
            d_rim = mm(hal[b, :, HALF:], eye, TN)
            y_here = y_recv[b, 0:HALF, :].astype(f32)
            d_here = y_recv[b, HALF:, :].astype(f32)
            out_ref[rows, :] = (q_s[rows, :].astype(f32) * y_here).astype(bf)
            y_wide = jnp.concatenate([y_here, y_rim], axis=1)
            d_wide = jnp.concatenate([d_here, d_rim], axis=1)
            for c in range(3):
                if c == 0:
                    grads = d_s[rows, :].astype(f32) * y_wide
                elif c == 1:
                    grads = d_wide * v_s[rows, :].astype(f32)
                else:
                    grads = d_wide * k_s[rows, :].astype(f32)
                acc = par[:, 3 * c : 3 * c + 1] * grads[:, :span]
                for j in (1, 2):
                    moved = pltpu.roll(grads, wide - j, 1)[:, :span]
                    acc = acc + par[:, 3 * c + j : 3 * c + j + 1] * moved * keep_s[j - 1, 0:1, :]
                df_ref[c, rows, :] = acc.astype(bf)

    def at(step, lag, work, only=None):
        b = step - lag
        ready = (b >= 0) & (b < blocks)

        @pl.when(ready if only is None else ready & only)
        def _():
            work(b)

    def advance(step, carry):
        at(step, 3, relay, inner)
        at(step, 0, prepare)
        at(step, 4, collect, inner)
        at(step, 5, transform, inner)
        at(step, 5, halo_send)
        at(step, 6, finish)

        @pl.when((step == 2) & inner)
        def _():
            lax.fori_loop(0, length // FINE, build, 0)

        return carry

    lax.fori_loop(0, blocks + 6, advance, 0)

    @pl.when(rank < n - 1)
    def _():
        rim_copy(0, rank).wait_send()

    @pl.when(rank > 0)
    def _():
        rim_copy(1, rank).wait_send()

    def drain(b, carry):
        @pl.when(rank > 0)
        def _():
            hal_copy(b, rank).wait_send()

        @pl.when(outer)
        def _():
            fwd_copy(b).wait_send()

        @pl.when(inner)
        def _():
            far_copy(b).wait_send()
            y_copy(b).wait_send()

        @pl.when(inner & own(b))
        def _():
            filt_copy(b).wait_send()
            twin_copy(b).wait_send()

        return carry

    lax.fori_loop(0, blocks, drain, 0)


def local_kernel(features, dout, filters, taps, skip, lengths):
    n = lax.axis_size("seq")
    channels, span = dout.shape
    blocks = channels // HALF
    length = n * span
    wide = span + 128
    bf = jnp.bfloat16
    par = jnp.concatenate([taps.reshape(9, channels), skip[None]], axis=0).T
    tab = jnp.asarray(np.stack(angle_parts(length)))
    vmem = pl.BlockSpec(memory_space=pltpu.VMEM)
    dma = pltpu.SemaphoreType.DMA
    return pl.pallas_call(
        functools.partial(mixer_kernel, n),
        out_shape=(
            jax.ShapeDtypeStruct(dout.shape, bf),
            jax.ShapeDtypeStruct(features.shape, bf),
        ),
        in_specs=[pl.BlockSpec(memory_space=pltpu.SMEM)] + [vmem] * 5,
        out_specs=(vmem, vmem),
        scratch_shapes=[
            pltpu.VMEM((16, channels), bf),
            pltpu.VMEM((32, channels), bf),
            pltpu.VMEM((3, span, wide), bf),
            pltpu.VMEM((4, 3, 32, wide), bf),
            pltpu.VMEM((2, 8, span), jnp.float32),
            pltpu.VMEM((channels, span), bf),
            pltpu.VMEM((channels, wide), bf),
            pltpu.VMEM((channels, wide), bf),
            pltpu.VMEM((channels, wide), bf),
            pltpu.VMEM((blocks, 3 * HALF, span), bf),
            pltpu.VMEM((blocks, 3 * HALF, length), bf),
            pltpu.VMEM((length, 2 * length), bf),
            pltpu.VMEM((2 * HALF, 2 * length), bf),
            pltpu.VMEM((blocks, 2 * HALF, span), bf),
            pltpu.VMEM((blocks, 2 * HALF, span), bf),
            pltpu.VMEM((blocks, 16, 2 * HALF), bf),
            pltpu.VMEM((blocks, 16, 2 * HALF), bf),
            dma((2,)), dma((2,)),
            dma((blocks,)), dma((blocks,)),
            dma((blocks,)), dma((blocks,)),
            dma((blocks,)), dma((blocks,)),
            dma((blocks,)), dma((blocks,)),
            dma((blocks,)), dma((blocks,)),
            dma((blocks,)), dma((blocks,)),
        ],
        compiler_params=pltpu.CompilerParams(
            collective_id=0, has_side_effects=True, vmem_limit_bytes=56 * 1024 * 1024
        ),
    )(lengths, features, dout, filters, par, tab)


def local(features, dout, filters, taps, skip, lengths):
    blocks = lax.axis_size("seq")
    channels, span = dout.shape
    fits = blocks == 4 and lax.axis_size("groups") == 2 and blocks * span <= DENSE_MAX and taps.shape[1] == 3
    if fits and span % 128 == 0 and channels % HALF == 0:
        return local_kernel(features, dout, filters, taps, skip, lengths)
    return local_general(features, dout, filters, taps, skip, lengths)


def solution(mesh):
    in_specs = (
        P(None, ("chan", "sub"), ("groups", "seq")),
        P(("chan", "sub"), ("groups", "seq")),
        P(("chan", "sub"), "seq"),
        P(None, None, ("chan", "sub")),
        P(("chan", "sub")),
        P("groups"),
    )
    out_specs = (P(("chan", "sub"), ("groups", "seq")), P(None, ("chan", "sub"), ("groups", "seq")))
    return jax.shard_map(local, mesh=mesh, in_specs=in_specs, out_specs=out_specs, check_vma=False)
```

```python
import functools

import jax
import numpy as np
import jax.numpy as jnp
from jax import lax
from jax.experimental import pallas as pl
from jax.experimental.pallas import tpu as pltpu
from jax.sharding import PartitionSpec as P

HIGHEST = lax.Precision.HIGHEST
TWO_PI = 6.283185307179586


def shifted(value, axis, steps):
    count = lax.axis_size(axis)
    leading, last = (max(0, -steps), min(count, count - steps))
    return lax.ppermute(value, axis, [(source, source + steps) for source in range(leading, last)])


def genome_offsets(lengths, positions):
    ends_at = jnp.cumsum(lengths, dtype=jnp.int32)
    before = (ends_at[None, :] <= positions[:, None]).astype(jnp.int32)
    return positions - jnp.sum(before * lengths[None, :], axis=1, dtype=jnp.int32)


def short_forward(extended, taps_local, offsets):
    span_rows = offsets.shape[0]
    count = taps_local.shape[1]
    result = jnp.zeros(extended.shape[:2] + (span_rows,), jnp.float32)
    for tap_index in range(count):
        begin = count - 1 - tap_index
        window = extended[:, :, begin : begin + span_rows].astype(jnp.float32)
        keep_mask = (offsets >= tap_index).astype(jnp.float32)
        result = result + taps_local[:, tap_index, :, None] * window * keep_mask[None, None, :]
    return result


def short_backward(grads_ext, taps_local, offsets_ext):
    count = taps_local.shape[1]
    span_rows = offsets_ext.shape[0] - (count - 1)
    result = jnp.zeros(grads_ext.shape[:2] + (span_rows,), jnp.float32)
    for tap_index in range(count):
        window = grads_ext[:, :, tap_index : tap_index + span_rows]
        keep_mask = (offsets_ext[tap_index : tap_index + span_rows] >= tap_index).astype(
            jnp.float32
        )
        result = result + taps_local[:, tap_index, :, None] * window * keep_mask[None, None, :]
    return result


def dft_table(rows_n, cols_n, period):
    row_ids = jnp.arange(rows_n, dtype=jnp.int32)
    col_ids = jnp.arange(cols_n, dtype=jnp.int32)
    phase = row_ids[:, None] * col_ids[None, :] % period
    angles = phase.astype(jnp.float32) * (-TWO_PI / period)
    return (jnp.cos(angles), jnp.sin(angles))


def forward_transform(signal, tables):
    (row_re, row_im), (twid_re, twid_im), (col_re, col_im) = tables
    half_rows = signal.shape[1] // 128
    blocks_in = signal.reshape(signal.shape[0], half_rows, 128)
    part_re = jnp.einsum("kn,cnm->ckm", row_re[:, :half_rows], blocks_in, precision=HIGHEST)
    part_im = jnp.einsum("kn,cnm->ckm", row_im[:, :half_rows], blocks_in, precision=HIGHEST)
    turned_re = part_re * twid_re - part_im * twid_im
    turned_im = part_re * twid_im + part_im * twid_re
    spec_re = jnp.einsum("ckn,nm->ckm", turned_re, col_re, precision=HIGHEST) - jnp.einsum(
        "ckn,nm->ckm", turned_im, col_im, precision=HIGHEST
    )
    spec_im = jnp.einsum("ckn,nm->ckm", turned_re, col_im, precision=HIGHEST) + jnp.einsum(
        "ckn,nm->ckm", turned_im, col_re, precision=HIGHEST
    )
    return (spec_re, spec_im)


def inverse_transform(spec_re, spec_im, tables):
    (row_re, row_im), (twid_re, twid_im), (col_re, col_im) = tables
    rows_n = spec_re.shape[1]
    half_rows = rows_n // 2
    mid_re = jnp.einsum("ckn,nm->ckm", spec_re, col_re, precision=HIGHEST) + jnp.einsum(
        "ckn,nm->ckm", spec_im, col_im, precision=HIGHEST
    )
    mid_im = jnp.einsum("ckn,nm->ckm", spec_im, col_re, precision=HIGHEST) - jnp.einsum(
        "ckn,nm->ckm", spec_re, col_im, precision=HIGHEST
    )
    back_re = mid_re * twid_re + mid_im * twid_im
    back_im = mid_im * twid_re - mid_re * twid_im
    signal = jnp.einsum("nk,ckm->cnm", row_re[:half_rows], back_re, precision=HIGHEST) + jnp.einsum(
        "nk,ckm->cnm", row_im[:half_rows], back_im, precision=HIGHEST
    )
    return signal.reshape(signal.shape[0], half_rows * 128) * (1.0 / (rows_n * 128))


def long_filter(filt, mixed_in, grad_in, skip_part):
    rows_n = 2 * mixed_in.shape[1] // 128
    tables = (
        dft_table(rows_n, rows_n, rows_n),
        dft_table(rows_n, 128, rows_n * 128),
        dft_table(128, 128, 128),
    )
    mixed_f = mixed_in.astype(jnp.float32)
    grad_f = grad_in.astype(jnp.float32)
    filt_re, filt_im = forward_transform(filt.astype(jnp.float32), tables)
    mix_re, mix_im = forward_transform(mixed_f, tables)
    grad_re, grad_im = forward_transform(grad_f, tables)
    conv_out = inverse_transform(
        filt_re * mix_re - filt_im * mix_im, filt_re * mix_im + filt_im * mix_re, tables
    )
    corr_out = inverse_transform(
        filt_re * grad_re + filt_im * grad_im, filt_re * grad_im - filt_im * grad_re, tables
    )
    y_out = (conv_out + skip_part[:, None] * mixed_f).astype(jnp.bfloat16)
    dmixed = (corr_out + skip_part[:, None] * grad_f).astype(jnp.bfloat16)
    return (y_out, dmixed)


DENSE_MAX = 1024
FINE = 32


def angle_parts(length):
    base = np.arange(length, dtype=np.int64) * 4 + 1
    fine = np.arange(FINE, dtype=np.int64)[:, None] * base[None, :] % (4 * length)
    coarse = np.arange(0, length, FINE, dtype=np.int64)[:, None] * base[None, :] % (4 * length)
    scale = 2.0 * np.pi / (4 * length)
    return [
        func(part * scale).astype(np.float32)
        for part in (coarse, fine)
        for func in (np.cos, np.sin)
    ]


def dense_filter(filt, mixed_in, grad_in, skip_part):
    length = mixed_in.shape[1]
    cc, cs, fc, fs = [jnp.asarray(p)[:, None] if i < 2 else jnp.asarray(p)[None] for i, p in enumerate(angle_parts(length))]
    cos_t = (cc * fc - cs * fs).reshape(length, length)
    sin_t = (cs * fc + cc * fs).reshape(length, length)
    table = jnp.concatenate([cos_t, sin_t], axis=1).astype(jnp.bfloat16)

    def fwd(x):
        return jnp.dot(x, table, preferred_element_type=jnp.float32)

    def inv(x):
        return lax.dot_general(x.astype(jnp.bfloat16), table, (((1,), (1,)), ((), ())), preferred_element_type=jnp.float32) * (1.0 / length)

    h, m, g = fwd(filt), fwd(mixed_in), fwd(grad_in)
    hc, hs = h[:, :length], h[:, length:]
    mc, ms = m[:, :length], m[:, length:]
    gc, gs = g[:, :length], g[:, length:]
    conv_out = inv(jnp.concatenate([hc * mc - hs * ms, hc * ms + hs * mc], axis=1))
    corr_out = inv(jnp.concatenate([hc * gc + hs * gs, hc * gs - hs * gc], axis=1))
    y_out = (conv_out + skip_part[:, None] * mixed_in.astype(jnp.float32)).astype(jnp.bfloat16)
    dmixed = (corr_out + skip_part[:, None] * grad_in.astype(jnp.float32)).astype(jnp.bfloat16)
    return (y_out, dmixed)


def to_channels(stacked):
    return lax.all_to_all(stacked, "seq", split_axis=1, concat_axis=2, tiled=True)


def to_sequence(stacked):
    return lax.all_to_all(stacked, "seq", split_axis=2, concat_axis=1, tiled=True)


def local_general(features, dout, filters, taps, skip, lengths):
    blocks = lax.axis_size("seq")
    seq_rank = lax.axis_index("seq")
    span_rows = features.shape[2]
    channels_here = features.shape[1]
    chan_part = channels_here // blocks
    count = taps.shape[1]
    margin = count - 1
    rim = shifted(features[:, :, span_rows - margin :], "seq", 1)
    extended = jnp.concatenate([rim, features], axis=2)
    first_pos = seq_rank * span_rows
    offsets = genome_offsets(lengths, first_pos + jnp.arange(span_rows, dtype=jnp.int32))
    filtered = short_forward(extended, taps, offsets).astype(jnp.bfloat16)
    query_side = filtered[0].astype(jnp.float32)
    key_side = filtered[1].astype(jnp.float32)
    value_side = filtered[2].astype(jnp.float32)
    dout_f = dout.astype(jnp.float32)
    mixed = (key_side * value_side).astype(jnp.bfloat16)
    grad_in = (dout_f * query_side).astype(jnp.bfloat16)
    moved = to_channels(jnp.stack([mixed, grad_in, filters]))
    skip_part = lax.dynamic_slice_in_dim(skip, seq_rank * chan_part, chan_part, 0)
    run = dense_filter if moved.shape[2] <= DENSE_MAX else long_filter
    y_out, dmixed = run(moved[2], moved[0], moved[1], skip_part)
    returned = to_sequence(jnp.stack([y_out, dmixed]))
    y_here = returned[0].astype(jnp.float32)
    dmixed_here = returned[1].astype(jnp.float32)
    out = (query_side * y_here).astype(jnp.bfloat16)
    grads = jnp.stack([dout_f * y_here, dmixed_here * value_side, dmixed_here * key_side])
    ahead = shifted(grads[:, :, :margin], "seq", -1)
    grads_ext = jnp.concatenate([grads, ahead], axis=2)
    offsets_ext = genome_offsets(
        lengths, first_pos + jnp.arange(span_rows + margin, dtype=jnp.int32)
    )
    dfeatures = short_backward(grads_ext, taps, offsets_ext).astype(jnp.bfloat16)
    return (out, dfeatures)


HALF = 256
NN = (((1,), (0,)), ((), ()))
NT = (((1,), (1,)), ((), ()))
TN = (((0,), (0,)), ((), ()))


def mm(a, b, dims=NN):
    return lax.dot_general(a, b, dims, preferred_element_type=jnp.float32)


def mixer_kernel(
    n,
    lengths_ref, feat_ref, dout_ref, filt_ref, par_ref, tab_ref,
    out_ref, df_ref,
    rim_src, rim, shift_m, place, keep_s, q_s, k_s, v_s, d_s,
    fwd_send, fwd_recv, table, spec, y_send, y_recv, hal_src, hal,
    rim_ss, rim_rs, fwd_ss, fwd_rs, far_ss, far_rs, filt_ss, filt_rs, twin_ss, twin_rs,
    y_ss, y_rs, hal_ss, hal_rs,
):
    rank = lax.axis_index("seq")
    span = feat_ref.shape[2]
    blocks = feat_ref.shape[1] // HALF
    length = span * n
    half = length // 2
    wide = span + 128
    bf = jnp.bfloat16
    f32 = jnp.float32
    group = lax.axis_index("groups")
    side = rank // 2
    inner = (rank == 1) | (rank == 2)
    outer = (rank == 0) | (rank == 3)
    middle = 1 + side
    edge = 3 * side
    across = 2 - side
    near = pl.ds(pl.multiple_of(side * half, 128), half)
    far = pl.ds(pl.multiple_of((1 - side) * half, 128), half)
    mine = pl.ds(pl.multiple_of(rank * span, 128), span)

    def peer(step):
        return lax.rem(rank + 1 + step, n)

    barrier = pltpu.get_barrier_semaphore()
    for step in range(n - 1):
        pl.semaphore_signal(barrier, inc=1, device_id={"seq": peer(step)}, device_id_type=pl.DeviceIdType.MESH)
    pl.semaphore_signal(barrier, inc=1, device_id={"groups": 1 - group}, device_id_type=pl.DeviceIdType.MESH)

    def remote(src, dst, ss, rs, dest):
        return pltpu.make_async_remote_copy(
            src_ref=src, dst_ref=dst, send_sem=ss, recv_sem=rs,
            device_id={"seq": dest}, device_id_type=pl.DeviceIdType.MESH,
        )

    def rim_copy(side, dest):
        return remote(rim_src, rim.at[pl.ds(16 * side, 16)], rim_ss.at[side], rim_rs.at[side], dest)

    def fwd_copy(b):
        return remote(fwd_send.at[b], fwd_recv.at[b, :, mine], fwd_ss.at[b], fwd_rs.at[b], middle)

    def far_copy(b):
        rows = pl.ds(pl.multiple_of(side * HALF, HALF), HALF)
        return remote(fwd_recv.at[b, rows, near], fwd_recv.at[b, rows, near], far_ss.at[b], far_rs.at[b], across)

    def filt_copy(b):
        rows = pl.ds(2 * HALF, HALF)
        return remote(fwd_recv.at[b, rows, near], fwd_recv.at[b, rows, near], filt_ss.at[b], filt_rs.at[b], across)

    def twin_copy(b):
        part = fwd_recv.at[b, pl.ds(2 * HALF, HALF), far]
        return pltpu.make_async_remote_copy(
            src_ref=part, dst_ref=part, send_sem=twin_ss.at[b], recv_sem=twin_rs.at[b],
            device_id={"groups": 1 - group}, device_id_type=pl.DeviceIdType.MESH,
        )

    def y_copy(b):
        return remote(y_send.at[b], y_recv.at[b], y_ss.at[b], y_rs.at[b], edge)

    def hal_copy(b, dest):
        return remote(hal_src.at[b], hal.at[b], hal_ss.at[b], hal_rs.at[b], dest)

    r_id = lax.broadcasted_iota(jnp.int32, (16, span), 0)
    p_id = lax.broadcasted_iota(jnp.int32, (16, span), 1)
    total = None
    for a in range(4):
        hit = (
            ((r_id == 4 * a) & (p_id == span - 2)) | ((r_id == 4 * a + 1) & (p_id == span - 1))
            | ((r_id == 4 * a + 2) & (p_id == 0)) | ((r_id == 4 * a + 3) & (p_id == 1))
        )
        pick = jnp.where(hit, 1.0, 0.0).astype(bf)
        term = mm(pick, feat_ref[a] if a < 3 else dout_ref[...], NT)
        total = term if total is None else total + term
    rim_src[...] = total.astype(bf)

    @pl.when(rank == 0)
    def _():
        rim[0:16, :] = jnp.zeros((16, rim.shape[1]), bf)

    @pl.when(rank == n - 1)
    def _():
        rim[16:32, :] = jnp.zeros((16, rim.shape[1]), bf)
        hal[...] = jnp.zeros(hal.shape, bf)

    @pl.when(inner)
    def _():
        rows = pl.ds(pl.multiple_of(side * HALF, HALF), HALF)
        for b in range(blocks):
            fwd_recv[b, rows, far] = jnp.zeros((HALF, half), bf)

    pl.semaphore_wait(barrier, n)

    @pl.when(rank < n - 1)
    def _():
        rim_copy(0, rank + 1).start()

    @pl.when(rank > 0)
    def _():
        rim_copy(1, rank - 1).start()

    def offsets_of(ahead, width):
        position = rank * span + ahead + lax.broadcasted_iota(jnp.int32, (8, width), 1)
        result = position
        end = jnp.int32(0)
        for g in range(lengths_ref.shape[0]):
            one = lengths_ref[g]
            end = end + one
            result = result - jnp.where(end <= position, one, 0)
        return result

    off_wide = offsets_of(0, wide)
    keep_s[0] = jnp.where(offsets_of(1, span) >= 1, 1.0, 0.0)
    keep_s[1] = jnp.where(offsets_of(2, span) >= 2, 1.0, 0.0)
    src_id = lax.broadcasted_iota(jnp.int32, (span, wide), 0)
    dst_id = lax.broadcasted_iota(jnp.int32, (span, wide), 1)
    row_id = lax.broadcasted_iota(jnp.int32, (32, wide), 0)
    col_id = lax.broadcasted_iota(jnp.int32, (32, wide), 1)
    for j in range(3):
        keep = jnp.where(off_wide >= j, 1.0, 0.0)[0:1, :]
        shift_m[j] = (jnp.where(dst_id - j == src_id, 1.0, 0.0) * keep).astype(bf)
        for a in range(4):
            hit = (
                ((row_id == 4 * a) & (col_id - j == -2)) | ((row_id == 4 * a + 1) & (col_id - j == -1))
                | ((row_id == 16 + 4 * a + 2) & (col_id - j == span))
                | ((row_id == 16 + 4 * a + 3) & (col_id - j == span + 1))
            )
            place[a, j] = (jnp.where(hit, 1.0, 0.0) * keep).astype(bf)

    @pl.when(rank > 0)
    def _():
        rim_copy(0, rank).wait_recv()

    @pl.when(rank < n - 1)
    def _():
        rim_copy(1, rank).wait_recv()

    def prepare(b):
        rows = pl.ds(pl.multiple_of(b * HALF, HALF), HALF)
        rim_part = rim[:, rows]
        par = par_ref[rows, :]

        def shifted_in(a, j):
            source = feat_ref[a, rows, :] if a < 3 else dout_ref[rows, :]
            return mm(source, shift_m[j]) + mm(rim_part, place[a, j], TN)

        result = []
        for a in range(3):
            acc = par[:, 3 * a : 3 * a + 1] * shifted_in(a, 0)
            acc = acc + par[:, 3 * a + 1 : 3 * a + 2] * shifted_in(a, 1)
            acc = acc + par[:, 3 * a + 2 : 3 * a + 3] * shifted_in(a, 2)
            result.append(acc.astype(bf))
        d_wide = shifted_in(3, 0).astype(bf)
        q_s[rows, :] = result[0][:, :span]
        k_s[rows, :] = result[1]
        v_s[rows, :] = result[2]
        d_s[rows, :] = d_wide
        mixed = (result[1][:, :span].astype(f32) * result[2][:, :span].astype(f32)).astype(bf)
        grad_in = (d_wide[:, :span].astype(f32) * result[0][:, :span].astype(f32)).astype(bf)

        @pl.when(outer)
        def _():
            fwd_send[b, 0:HALF, :] = mixed
            fwd_send[b, HALF : 2 * HALF, :] = grad_in
            fwd_send[b, 2 * HALF :, :] = filt_ref[rows, :]
            fwd_copy(b).start()

        @pl.when(inner)
        def _():
            fwd_recv[b, 0:HALF, mine] = mixed
            fwd_recv[b, HALF : 2 * HALF, mine] = grad_in
            fwd_recv[b, 2 * HALF :, mine] = filt_ref[rows, :]

    def own(b):
        return lax.rem(b, 2) == group

    def relay(b):
        fwd_copy(b).wait_recv()
        far_copy(b).start()

        @pl.when(own(b))
        def _():
            filt_copy(b).start()

    def collect(b):
        far_copy(b).wait_recv()

        @pl.when(own(b))
        def _():
            filt_copy(b).wait_recv()
            twin_copy(b).start()

    fine_c = tab_ref[2]
    fine_s = tab_ref[3]

    def build(a, carry):
        big_c = tab_ref[0, pl.ds(a, 1), :]
        big_s = tab_ref[1, pl.ds(a, 1), :]
        rows = pl.ds(pl.multiple_of(a * FINE, FINE), FINE)
        table[rows, 0:length] = (big_c * fine_c - big_s * fine_s).astype(bf)
        table[rows, length:] = (big_s * fine_c + big_c * fine_s).astype(bf)
        return carry

    tile = 256

    def transform(b):
        @pl.when(jnp.logical_not(own(b)))
        def _():
            twin_copy(b).wait_recv()

        def spectrum_tile(t, carry):
            cols = pl.ds(pl.multiple_of(t * tile, tile), tile)
            sins = pl.ds(pl.multiple_of(length + t * tile, tile), tile)
            signal = fwd_recv[b]
            x_c = mm(signal, table[:, cols])
            x_s = mm(signal, table[:, sins])
            h_c = x_c[2 * HALF :]
            h_s = x_s[2 * HALF :]
            m_c, g_c = x_c[:HALF], x_c[HALF : 2 * HALF]
            m_s, g_s = x_s[:HALF], x_s[HALF : 2 * HALF]
            spec[0:HALF, cols] = (h_c * m_c - h_s * m_s).astype(bf)
            spec[0:HALF, sins] = (h_c * m_s + h_s * m_c).astype(bf)
            spec[HALF:, cols] = (h_c * g_c + h_s * g_s).astype(bf)
            spec[HALF:, sins] = (h_c * g_s - h_s * g_c).astype(bf)
            return carry

        lax.fori_loop(0, length // tile, spectrum_tile, 0)
        skip_col = par_ref[pl.ds(pl.multiple_of(b * HALF, HALF), HALF), 9:10]

        def results(dest):
            cols = pl.ds(pl.multiple_of(dest * span, 128), span)
            value = mm(spec[...], table[cols, :], NT) * (1.0 / length)
            signal = fwd_recv[b, 0 : 2 * HALF, cols].astype(f32)
            y_part = (value[:HALF] + skip_col * signal[:HALF]).astype(bf)
            d_part = (value[HALF:] + skip_col * signal[HALF:]).astype(bf)
            return y_part, d_part

        y_part, d_part = results(edge)
        y_send[b, 0:HALF, :] = y_part
        y_send[b, HALF:, :] = d_part
        y_copy(b).start()
        y_part, d_part = results(rank)
        y_recv[b, 0:HALF, :] = y_part
        y_recv[b, HALF:, :] = d_part

    r_id = lax.broadcasted_iota(jnp.int32, (16, 128), 0)
    c_id = lax.broadcasted_iota(jnp.int32, (16, 128), 1)
    eye = jnp.where((r_id == c_id) & (r_id < 2), 1.0, 0.0).astype(bf)

    def halo_send(b):
        @pl.when(outer)
        def _():
            y_copy(b).wait_recv()

        hal_src[b] = mm(eye, y_recv[b, :, 0:128], NT).astype(bf)

        @pl.when(rank > 0)
        def _():
            hal_copy(b, rank - 1).start()

    def finish(b):
        @pl.when(rank < n - 1)
        def _():
            hal_copy(b, rank).wait_recv()

        if True:
            rows = pl.ds(pl.multiple_of(b * HALF, HALF), HALF)
            par = par_ref[rows, :]
            y_rim = mm(hal[b, :, 0:HALF], eye, TN)
            d_rim = mm(hal[b, :, HALF:], eye, TN)
            y_here = y_recv[b, 0:HALF, :].astype(f32)
            d_here = y_recv[b, HALF:, :].astype(f32)
            out_ref[rows, :] = (q_s[rows, :].astype(f32) * y_here).astype(bf)
            y_wide = jnp.concatenate([y_here, y_rim], axis=1)
            d_wide = jnp.concatenate([d_here, d_rim], axis=1)
            for c in range(3):
                if c == 0:
                    grads = d_s[rows, :].astype(f32) * y_wide
                elif c == 1:
                    grads = d_wide * v_s[rows, :].astype(f32)
                else:
                    grads = d_wide * k_s[rows, :].astype(f32)
                acc = par[:, 3 * c : 3 * c + 1] * grads[:, :span]
                for j in (1, 2):
                    moved = pltpu.roll(grads, wide - j, 1)[:, :span]
                    acc = acc + par[:, 3 * c + j : 3 * c + j + 1] * moved * keep_s[j - 1, 0:1, :]
                df_ref[c, rows, :] = acc.astype(bf)

    def at(step, lag, work, only=None):
        b = step - lag
        ready = (b >= 0) & (b < blocks)

        @pl.when(ready if only is None else ready & only)
        def _():
            work(b)

    def advance(step, carry):
        at(step, 2, relay, inner)
        at(step, 0, prepare)
        at(step, 3, collect, inner)
        at(step, 3, transform, inner)
        at(step, 3, halo_send)
        at(step, 4, finish)

        @pl.when((step == 1) & inner)
        def _():
            lax.fori_loop(0, length // FINE, build, 0)

        return carry

    lax.fori_loop(0, blocks + 4, advance, 0)

    @pl.when(rank < n - 1)
    def _():
        rim_copy(0, rank).wait_send()

    @pl.when(rank > 0)
    def _():
        rim_copy(1, rank).wait_send()

    def drain(b, carry):
        @pl.when(rank > 0)
        def _():
            hal_copy(b, rank).wait_send()

        @pl.when(outer)
        def _():
            fwd_copy(b).wait_send()

        @pl.when(inner)
        def _():
            far_copy(b).wait_send()
            y_copy(b).wait_send()

        @pl.when(inner & own(b))
        def _():
            filt_copy(b).wait_send()
            twin_copy(b).wait_send()

        return carry

    lax.fori_loop(0, blocks, drain, 0)


def local_kernel(features, dout, filters, taps, skip, lengths):
    n = lax.axis_size("seq")
    channels, span = dout.shape
    blocks = channels // HALF
    length = n * span
    wide = span + 128
    bf = jnp.bfloat16
    par = jnp.concatenate([taps.reshape(9, channels), skip[None]], axis=0).T
    tab = jnp.asarray(np.stack(angle_parts(length)))
    vmem = pl.BlockSpec(memory_space=pltpu.VMEM)
    dma = pltpu.SemaphoreType.DMA
    return pl.pallas_call(
        functools.partial(mixer_kernel, n),
        out_shape=(
            jax.ShapeDtypeStruct(dout.shape, bf),
            jax.ShapeDtypeStruct(features.shape, bf),
        ),
        in_specs=[pl.BlockSpec(memory_space=pltpu.SMEM)] + [vmem] * 5,
        out_specs=(vmem, vmem),
        scratch_shapes=[
            pltpu.VMEM((16, channels), bf),
            pltpu.VMEM((32, channels), bf),
            pltpu.VMEM((3, span, wide), bf),
            pltpu.VMEM((4, 3, 32, wide), bf),
            pltpu.VMEM((2, 8, span), jnp.float32),
            pltpu.VMEM((channels, span), bf),
            pltpu.VMEM((channels, wide), bf),
            pltpu.VMEM((channels, wide), bf),
            pltpu.VMEM((channels, wide), bf),
            pltpu.VMEM((blocks, 3 * HALF, span), bf),
            pltpu.VMEM((blocks, 3 * HALF, length), bf),
            pltpu.VMEM((length, 2 * length), bf),
            pltpu.VMEM((2 * HALF, 2 * length), bf),
            pltpu.VMEM((blocks, 2 * HALF, span), bf),
            pltpu.VMEM((blocks, 2 * HALF, span), bf),
            pltpu.VMEM((blocks, 16, 2 * HALF), bf),
            pltpu.VMEM((blocks, 16, 2 * HALF), bf),
            dma((2,)), dma((2,)),
            dma((blocks,)), dma((blocks,)),
            dma((blocks,)), dma((blocks,)),
            dma((blocks,)), dma((blocks,)),
            dma((blocks,)), dma((blocks,)),
            dma((blocks,)), dma((blocks,)),
            dma((blocks,)), dma((blocks,)),
        ],
        compiler_params=pltpu.CompilerParams(
            collective_id=0, has_side_effects=True, vmem_limit_bytes=56 * 1024 * 1024
        ),
    )(lengths, features, dout, filters, par, tab)


def local(features, dout, filters, taps, skip, lengths):
    blocks = lax.axis_size("seq")
    channels, span = dout.shape
    fits = blocks == 4 and lax.axis_size("groups") == 2 and blocks * span <= DENSE_MAX and taps.shape[1] == 3
    if fits and span % 128 == 0 and channels % HALF == 0:
        return local_kernel(features, dout, filters, taps, skip, lengths)
    return local_general(features, dout, filters, taps, skip, lengths)


def solution(mesh):
    in_specs = (
        P(None, ("chan", "sub"), ("groups", "seq")),
        P(("chan", "sub"), ("groups", "seq")),
        P(("chan", "sub"), "seq"),
        P(None, None, ("chan", "sub")),
        P(("chan", "sub")),
        P("groups"),
    )
    out_specs = (P(("chan", "sub"), ("groups", "seq")), P(None, ("chan", "sub"), ("groups", "seq")))
    return jax.shard_map(local, mesh=mesh, in_specs=in_specs, out_specs=out_specs, check_vma=False)
```
